128 devices in a mesh: row: 16 (over y, z), col: 8 (over x, core).
Axes of the slice: x: 4, y: 4, z: 4, core: 2. Of those that a mesh axis runs over, the one named last changes fastest.
Arguments:
- a_blocks: bfloat16 [16, 4096, 4096], P('col', 'row'), may hold values from -0.19921875 to 0.19921875
- a_row: int32 [16, 4096], P(None, 'row'), may hold values from 0 to 31
- a_col: int32 [16, 4096], P(None, 'row'), may hold values from 0 to 15
- p_blocks: bfloat16 [16, 1024, 4096], P('row', 'col'), may hold values from -6 to 6
- p_row: int32 [16, 1024], P(None, 'col'), may hold values from 0 to 15
- p_col: int32 [16, 1024], P(None, 'col'), may hold values from 0 to 15
- q_blocks: bfloat16 [512, 4096], P('row'), may hold values from -0.75 to 0.75
- sched: int32 [2], replicated, may hold values from 0 to 15, as said below
- fine_agg: int32 [512], replicated, may hold values from 0 to 63, as said below
- coarse_place: int32 [64], replicated, may hold values from 0 to 63, as said below
- prod_cols: int32 [512, 64], P(None, 'col'), may hold values from 0 to 15, as said below
Outputs:
- coarse: float32 [4096, 8192], P('row', 'col')
The draws below stay inside these ranges and needn't reach their ends.
Inputs may be any that keep to these rules, and one draw needn't show every extreme that they name: `sched`: the 2 panels are distinct, and one of them is the last panel. `fine_agg`: aggregate a belongs to owner coarse_place[a] // 4. Of the 32 fine block rows of one row group (rows i * 32 to i * 32 + 31) at most 10 lie in aggregates of one owner, and in every row group some owner has exactly 10. `coarse_place`: A permutation of the aggregates. `prod_cols`: the 8 entries of row g for column group j (entries j * 8 to j * 8 + 7) are distinct.
All inputs are finite; a program needn't handle non-finite values.
Results may differ from the reference program's by a relative error of at most 0.004.
Values may be sent and summed in bfloat16 or wider, within the bound.
A program may use at most 192 MiB of HBM per device.

```python
import jax
import jax.numpy as jnp
from jax import lax

B = 64
FR = 32
KB = 16
CB = 16
CPR = 8
NA = 256
NP = 128
AGG_DEV = 4
SECTIONS = 2
PANELS = 16
COLGROUPS = 8
FB = 512
NAGG = 64
NCB = 128
N_ROW = 16
N_COL = 8


def owner_maps(key):
    place_key = jax.random.fold_in(key, 11)
    order_key = jax.random.fold_in(key, 12)
    owner_key = jax.random.fold_in(key, 13)
    member_key = jax.random.fold_in(key, 14)
    placing = jax.random.permutation(place_key, NAGG).astype(jnp.int32)
    inverse = jnp.argsort(placing).astype(jnp.int32)
    order_scores = jax.random.randint(order_key, (PANELS, FR), 0, 1 << 20) * FR + jnp.arange(FR, dtype=jnp.int32)[None, :]
    position = jnp.argsort(jnp.argsort(order_scores, axis=1), axis=1).astype(jnp.int32)
    quarter = FR // 4
    rank_of_row = jnp.where(position < quarter, 0, (position - quarter) % PANELS).astype(jnp.int32)
    owner_scores = jax.random.randint(owner_key, (PANELS, PANELS), 0, 1 << 20) * PANELS + jnp.arange(PANELS, dtype=jnp.int32)[None, :]
    owner_perm = jnp.argsort(owner_scores, axis=1).astype(jnp.int32)
    owners = jnp.take_along_axis(owner_perm, rank_of_row, axis=1)
    member = jax.random.randint(member_key, (PANELS, FR), 0, AGG_DEV).astype(jnp.int32)
    fine = inverse[(owners * AGG_DEV + member).reshape(-1)]
    return (placing, fine.astype(jnp.int32))


def draw_fine_agg(key, part):
    return owner_maps(key)[1]


def draw_coarse_place(key, part):
    return owner_maps(key)[0]


def draw_sched(key, part):
    order = jax.random.permutation(jax.random.fold_in(key, 21), PANELS).astype(jnp.int32)
    chosen = order[:SECTIONS]
    biggest = jnp.argmax(chosen)
    chosen = chosen.at[biggest].set(PANELS - 1)
    return chosen.astype(jnp.int32)


def draw_prod_cols(key, part):
    scores = jax.random.randint(key, (FB, COLGROUPS, CB), 0, 1 << 20) * CB + jnp.arange(CB, dtype=jnp.int32)
    chosen = jnp.argsort(scores, axis=2)[:, :, :CPR]
    return chosen.reshape(FB, COLGROUPS * CPR).astype(jnp.int32)


def plant(array, stream_key, least, high):
    spot = [jax.random.randint(jax.random.fold_in(stream_key, axis), (), 0, length) for axis, length in enumerate(array.shape)]
    longest = array.shape.index(max(array.shape))
    neighbour = spot[:longest] + [(spot[longest] + 1) % array.shape[longest]] + spot[longest + 1:]
    return array.at[tuple(spot)].set(least).at[tuple(neighbour)].set(high)


def block_levels(rng, shape, pieces, least, largest):
    gain, own = 1.0, jax.random.fold_in(rng, 6)
    for dim, parts in pieces:
        steps = jnp.exp(jax.random.uniform(jax.random.fold_in(own, dim), (parts,), jnp.float32, least / len(pieces), largest / len(pieces)))
        gain = gain * jnp.repeat(steps, shape[dim] // parts).reshape([-1 if axis == dim else 1 for axis in range(len(shape))])
    return gain


def gaussian(own_key, dims, scale, most, pieces=(), kind=jnp.bfloat16):
    drawn = jax.random.normal(own_key, dims, jnp.float32) * scale
    if len(pieces) > 0:
        drawn = block_levels(own_key, dims, pieces, -0.22, 0.18) * drawn
    return jnp.clip(drawn, min=-most, max=most).astype(kind)


def setup_inputs(seed: int = 0) -> dict:
    key_list = jax.random.split(jax.random.key(seed), 12)
    a_blocks = gaussian(key_list[0], (PANELS, N_ROW * NA, B * B), 0.03125, 0.19921875, ((0, 8), (1, 16)))
    a_row = plant(jax.random.randint(key_list[1], (PANELS, N_ROW * NA), 0, FR), jax.random.fold_in(key_list[1], 1), 0, FR - 1).astype(jnp.int32)
    a_col = plant(jax.random.randint(key_list[2], (PANELS, N_ROW * NA), 0, KB), jax.random.fold_in(key_list[2], 1), 0, KB - 1).astype(jnp.int32)
    p_blocks = gaussian(key_list[3], (PANELS, N_COL * NP, B * B), 1.0, 6.0, ((0, 16), (1, 8)))
    p_row = plant(jax.random.randint(key_list[4], (PANELS, N_COL * NP), 0, KB), jax.random.fold_in(key_list[4], 1), 0, KB - 1).astype(jnp.int32)
    p_col = plant(jax.random.randint(key_list[5], (PANELS, N_COL * NP), 0, CB), jax.random.fold_in(key_list[5], 1), 0, CB - 1).astype(jnp.int32)
    q_blocks = gaussian(key_list[6], (FB, B * B), B ** -0.5, 0.75, ((0, 16),))
    sched = draw_sched(jax.random.fold_in(key_list[11], 71), 0)
    fine_agg = draw_fine_agg(jax.random.fold_in(key_list[11], 71), 0)
    coarse_place = draw_coarse_place(jax.random.fold_in(key_list[11], 71), 0)
    prod_cols = draw_prod_cols(jax.random.fold_in(key_list[11], 71), 0)
    return dict(a_blocks=a_blocks, a_row=a_row, a_col=a_col, p_blocks=p_blocks, p_row=p_row, p_col=p_col, q_blocks=q_blocks, sched=sched, fine_agg=fine_agg, coarse_place=coarse_place, prod_cols=prod_cols)


def dense_panel(blocks, block_rows, block_cols, height, breadth):
    tiles = blocks.reshape(blocks.shape[0], B, B).astype(jnp.float32)
    grid_sum = jnp.zeros((height, breadth, B, B), jnp.float32).at[block_rows, block_cols].add(tiles)
    return grid_sum.transpose(0, 2, 1, 3).reshape(height * B, breadth * B).astype(jnp.bfloat16)


def reference(a_blocks, a_row, a_col, p_blocks, p_row, p_col, q_blocks, sched, fine_agg, coarse_place, prod_cols):
    zero_index = jnp.zeros((), jnp.int32)
    column_offset = (jnp.arange(COLGROUPS * NP, dtype=jnp.int32) // NP) * CB
    p_panels = []
    for section in range(SECTIONS):
        panel_id = sched[section]
        p_panels.append(dense_panel(p_blocks[panel_id], p_row[panel_id], p_col[panel_id] + column_offset, KB, NCB))

    def one_group(totals, group):
        row_start = (group * FR).astype(jnp.int32)
        start_a = (group * NA).astype(jnp.int32)
        product = jnp.zeros((FR * B, NCB * B), jnp.float32)
        for section in range(SECTIONS):
            panel_id = sched[section]
            blocks = lax.dynamic_slice(a_blocks, (panel_id, start_a, zero_index), (1, NA, B * B))[0]
            block_rows = lax.dynamic_slice_in_dim(a_row[panel_id], start_a, NA, 0)
            block_cols = lax.dynamic_slice_in_dim(a_col[panel_id], start_a, NA, 0)
            panel = dense_panel(blocks, block_rows, block_cols, FR, KB)
            product = product + jnp.dot(panel, p_panels[section], preferred_element_type=jnp.float32)
        picked_cols = lax.dynamic_slice_in_dim(prod_cols, row_start, FR, 0).reshape(FR, COLGROUPS, CPR)
        blocked = product.reshape(FR, B, COLGROUPS, CB, B)
        picked = jnp.take_along_axis(blocked, picked_cols[:, None, :, :, None], axis=3)
        restrict = lax.dynamic_slice_in_dim(q_blocks, row_start, FR, 0).reshape(FR, B, B).astype(jnp.float32)
        contrib = jnp.einsum("rxa,rxjqb->rajqb", restrict, picked, precision=lax.Precision.HIGHEST).astype(jnp.bfloat16)
        column_hot = (picked_cols[..., None] == jnp.arange(CB, dtype=jnp.int32)).astype(jnp.float32)
        spread = jnp.einsum("rjqc,rajqb->rajcb", column_hot, contrib.astype(jnp.float32), precision=lax.Precision.HIGHEST)
        placing = coarse_place[lax.dynamic_slice_in_dim(fine_agg, row_start, FR, 0)]
        totals = totals.at[placing].add(spread.reshape(FR, B, NCB * B))
        return totals, None

    totals, unused = lax.scan(one_group, jnp.zeros((NAGG, B, NCB * B), jnp.float32), jnp.arange(PANELS, dtype=jnp.int32))
    return totals.reshape(NAGG * B, NCB * B)
```

```python
import jax
import jax.numpy as jnp
from jax import lax
from jax.experimental import pallas as pl
from jax.experimental.pallas import tpu as pltpu
from jax.sharding import PartitionSpec as P

B = 64
FR = 32
KB = 16
CB = 16
SECTIONS = 2
LANES = 128


def from_root(x, axis, root):
    return lax.dynamic_index_in_dim(lax.all_gather(x, axis), root, 0, keepdims=False)


def from_root_2(value, axis, source):
    kept = jnp.where(lax.axis_index(axis) == source, value, 0).astype(value.dtype)
    return lax.psum(kept, axis)


def halves(x, odd):
    lane = lax.broadcasted_iota(jnp.int32, (x.shape[0], LANES), 1)
    is_odd = jnp.broadcast_to(odd, (x.shape[0], LANES)) == 1
    keep = (lane < 64) != is_odd
    evens, odds = [], []
    for part in range(2):
        own = x[:, part * LANES:(part + 1) * LANES].astype(jnp.float32)
        swapped = pltpu.roll(own, 64, 1)
        evens.append(jnp.where(keep, jnp.where(is_odd, swapped, own), 0.0).astype(jnp.bfloat16))
        odds.append(jnp.where(keep, jnp.where(is_odd, own, swapped), 0.0).astype(jnp.bfloat16))
    return jnp.concatenate(evens, axis=1), jnp.concatenate(odds, axis=1)


def one_hot(position, count):
    rows = lax.broadcasted_iota(jnp.int32, (count, position.shape[1]), 0)
    return jnp.where(rows == position, 1.0, 0.0).astype(jnp.bfloat16)


def dot(a, b):
    return jnp.dot(a, b, preferred_element_type=jnp.float32)


def local_kernel(place, a_ref, p_ref, a_pos, a_odd, p_pos, p_odd, q_ref, mask_ref, out_ref, a_dense, p_rows, p_dense, product):
    row_index = lax.broadcasted_iota(jnp.int32, (256, 256), 0)
    col_index = lax.broadcasted_iota(jnp.int32, (256, 256), 1)
    swap = jnp.where(col_index == (row_index % 16) * 16 + row_index // 16, 1.0, 0.0).astype(jnp.bfloat16)

    for s in range(SECTIONS):
        p_hot = one_hot(p_pos[s], 128)

        @pl.loop(0, 16)
        def _(q):
            lanes = pl.ds(pl.multiple_of(q * 256, 256), 256)
            parts = halves(p_ref[s, :, lanes], p_odd[s])
            for h in range(2):
                placed = dot(p_hot, parts[h]).astype(jnp.bfloat16)
                for part in range(2):
                    start = pl.multiple_of((q * 4 + part * 2 + h) * KB, KB)
                    for j in range(CB // 2):
                        p_rows[pl.ds(start, KB), j * LANES:(j + 1) * LANES] = placed[j * KB:(j + 1) * KB, part * LANES:(part + 1) * LANES]

        for group in range(4):
            ordered = dot(swap, p_rows[group * 256:(group + 1) * 256, :]).astype(jnp.bfloat16)
            for k in range(KB):
                start = s * KB * B + k * B + group * 16
                p_dense[start:start + 16, :] = ordered[k * 16:(k + 1) * 16, :]

    for s in range(SECTIONS):
        a_hot = one_hot(a_pos[s], 256)

        @pl.loop(0, 16)
        def _(q):
            lanes = pl.ds(pl.multiple_of(q * 256, 256), 256)
            parts = halves(a_ref[s, :, lanes], a_odd[s])
            for h in range(2):
                placed = dot(a_hot, parts[h]).astype(jnp.bfloat16)
                for part in range(2):
                    start = pl.multiple_of((q * 4 + part * 2 + h) * FR, FR)
                    for k in range(KB // 2):
                        lane = s * KB * B + k * LANES
                        a_dense[pl.ds(start, FR), lane:lane + LANES] = placed[k * FR:(k + 1) * FR, part * LANES:(part + 1) * LANES]

    for n in range(4):

        @pl.loop(0, 4)
        def _(m):
            start = pl.multiple_of(m * 512, 512)
            tile = dot(a_dense[pl.ds(start, 512), :], p_dense[:, n * 256:(n + 1) * 256])
            product[2 * n, pl.ds(start, 512), :] = tile[:, :LANES]
            product[2 * n + 1, pl.ds(start, 512), :] = tile[:, LANES:]

    @pl.loop(0, 64)
    def _(g):
        out_ref[pl.ds(pl.multiple_of(g * B, B), B), :] = jnp.zeros((B, CB * B), jnp.float32)

    @pl.loop(0, FR)
    def _(i):
        restrict = q_ref[i]
        lhs = jnp.concatenate([restrict, restrict], axis=1)
        rows = pl.ds(pl.multiple_of(place[i] * B, B), B)
        for j in range(0, 8, 2):
            tops, bottoms = [], []
            for t in (j, j + 1):
                block = product[t, pl.ds(i, B, stride=FR), :]
                top = block.astype(jnp.bfloat16)
                tops.append(top)
                bottoms.append((block - top.astype(jnp.float32)).astype(jnp.bfloat16))
            rhs = jnp.concatenate([jnp.concatenate(tops, axis=1), jnp.concatenate(bottoms, axis=1)], axis=0)
            term = dot(lhs, rhs).astype(jnp.bfloat16).astype(jnp.float32)
            lanes = slice(j * LANES, (j + 2) * LANES)
            out_ref[rows, lanes] += term * mask_ref[i, :, lanes]


def local_terms(a, p, a_row, a_col, p_row, p_col, q, place, picked_cols):
    a_pos = ((a_col // 2) * FR + a_row)[:, None, :]
    p_pos = ((p_col // 2) * KB + p_row)[:, None, :]
    a_odd = (a_col % 2)[:, :, None]
    p_odd = (p_col % 2)[:, :, None]
    hit = (picked_cols[:, :, None] == jnp.arange(CB, dtype=jnp.int32)).any(axis=1)
    mask = jnp.repeat(hit.astype(jnp.float32), B, axis=1)[:, None, :]
    q_t = q.reshape(FR, B, B).transpose(0, 2, 1)
    vmem = pl.BlockSpec(memory_space=pltpu.VMEM)
    return pl.pallas_call(
        local_kernel,
        out_shape=jax.ShapeDtypeStruct((64 * B, CB * B), jnp.float32),
        in_specs=[pl.BlockSpec(memory_space=pltpu.SMEM)] + [vmem] * 8,
        out_specs=vmem,
        scratch_shapes=[
            pltpu.VMEM((FR * B, SECTIONS * KB * B), jnp.bfloat16),
            pltpu.VMEM((KB * B, CB * B), jnp.bfloat16),
            pltpu.VMEM((SECTIONS * KB * B, CB * B), jnp.bfloat16),
            pltpu.VMEM((8, FR * B, LANES), jnp.float32),
        ],
        compiler_params=pltpu.CompilerParams(vmem_limit_bytes=60 * 1024 * 1024),
    )(place, a, p, a_pos, a_odd, p_pos, p_odd, q_t, mask)


def per_device(a_blocks, a_row, a_col, p_blocks, p_row, p_col, q_blocks, sched, fine_agg, coarse_place, prod_cols):
    panels_held = a_blocks.shape[0]
    own_row = lax.axis_index("row")
    a_parts, p_parts = [], []
    for section in range(SECTIONS):
        panel_id = sched[section]
        mine = lax.dynamic_index_in_dim(a_blocks, panel_id % panels_held, 0, keepdims=False)
        a_parts.append(from_root(mine, "col", panel_id // panels_held))
        p_parts.append(from_root_2(p_blocks[0], "row", panel_id))
    row_start = own_row * FR
    picked_cols = lax.dynamic_slice_in_dim(prod_cols, row_start, FR, 0)
    place = coarse_place[lax.dynamic_slice_in_dim(fine_agg, row_start, FR, 0)]
    term = local_terms(
        jnp.stack(a_parts), jnp.stack(p_parts), a_row[sched], a_col[sched], p_row[sched], p_col[sched], q_blocks, place, picked_cols
    )
    return lax.psum_scatter(term, "row", scatter_dimension=0, tiled=True)


def solution(mesh):
    in_specs = (
        P("col", "row", None),
        P(None, "row"),
        P(None, "row"),
        P("row", "col", None),
        P(None, "col"),
        P(None, "col"),
        P("row", None),
        P(),
        P(),
        P(),
        P(None, "col"),
    )
    return jax.shard_map(per_device, mesh=mesh, in_specs=in_specs, out_specs=P("row", "col"), check_vma=False)
```

```python
import functools

import jax
import jax.numpy as jnp
from jax import lax
from jax.experimental import pallas as pl
from jax.experimental.pallas import tpu as pltpu
from jax.sharding import PartitionSpec as P

B = 64
FR = 32
KB = 16
CB = 16
SECTIONS = 2
LANES = 128
AGG_DEV = 4


MESH = pl.DeviceIdType.MESH
LAST = 15
A_GROUPS = 16
P_GROUPS = 8


def remote(src, dst, send_sem, recv_sem, target):
    return pltpu.make_async_remote_copy(
        src_ref=src, dst_ref=dst, send_sem=send_sem, recv_sem=recv_sem, device_id=target, device_id_type=MESH
    )


def greet(targets):
    barrier = pltpu.get_barrier_semaphore()
    for target in targets:
        pl.semaphore_signal(barrier, inc=1, device_id=target, device_id_type=MESH)
    pl.semaphore_wait(barrier, len(targets))


def place_of():
    row, col = lax.axis_index("row"), lax.axis_index("col")
    return row // 4, row % 4, col // 2, col % 2


def device(y, z, x, core):
    return (y * 4 + z, x * 2 + core)


def gather_kernel(panel, a_ref, p_ref, a_out, p_out, a_buf, p_buf, a_recv, p_recv, a_fwd, a_sib, p_trunk, p_branch, load_sem, out_sem):
    y, z, x, core = place_of()
    sibling = device(y, z, x, 1 - core)
    x_next = [device(y, z, (x + 1) % 4, core), device(y, z, (x + 3) % 4, core)]
    y_next = [device((y + 1) % 4, z, x, core), device((y + 3) % 4, z, x, core)]
    z_next = [device(y, (z + 1) % 4, x, core), device(y, (z + 3) % 4, x, core)]
    greet([sibling] + x_next + y_next + z_next)
    panels = (LAST, panel)
    for s, k in enumerate(panels):
        x_root, core_root = (k // 2) // 2, (k // 2) % 2

        @pl.when((x == x_root) & (core == core_root))
        def _():
            pltpu.make_async_copy(a_ref.at[k % 2], a_buf.at[s], load_sem.at[0, s]).start()

        @pl.when((y == k // 4) & (z == k % 4))
        def _():
            pltpu.make_async_copy(p_ref.at[0], p_buf.at[s], load_sem.at[1, s]).start()

    for s, k in enumerate(panels):
        x_root, core_root = (k // 2) // 2, (k // 2) % 2

        @pl.when((x == x_root) & (core == core_root))
        def _():
            pltpu.make_async_copy(a_ref.at[k % 2], a_buf.at[s], load_sem.at[0, s]).wait()

        @pl.when((y == k // 4) & (z == k % 4))
        def _():
            pltpu.make_async_copy(p_ref.at[0], p_buf.at[s], load_sem.at[1, s]).wait()

    def a_stream(s, k, way, t):
        x_root, core_root = (k // 2) // 2, (k // 2) % 2
        ahead = (x - x_root + 4) % 4 if way == 0 else (x_root - x + 4) % 4
        active = core == core_root
        g = t - ahead - jnp.where(active, 0, 1)
        block = way * (A_GROUPS // 2) + g

        @pl.when((g >= 0) & (g < A_GROUPS // 2))
        def _():
            here = a_buf.at[s, block]

            @pl.when(jnp.logical_not(active & (ahead == 0)))
            def _():
                remote(here, here, a_fwd.at[s, way], a_recv.at[s, block], sibling).wait_recv()

            @pl.when(active & (ahead < 3))
            def _():
                remote(here, here, a_fwd.at[s, way], a_recv.at[s, block], x_next[way]).start()

            @pl.when(active)
            def _():
                remote(here, here, a_sib.at[s, way], a_recv.at[s, block], sibling).start()

            pltpu.make_async_copy(here, a_out.at[s, block], out_sem.at[0]).start()

    def p_stream(s, k, quarter, t):
        back = quarter % 2
        if quarter < 2:
            first, second, trunk, branch = (y, k // 4), (z, k % 4), y_next, z_next
        else:
            first, second, trunk, branch = (z, k % 4), (y, k // 4), z_next, y_next
        e1 = (first[0] - first[1] + 4) % 4 if back == 0 else (first[1] - first[0] + 4) % 4
        e2 = (second[0] - second[1] + 4) % 4 if back == 0 else (second[1] - second[0] + 4) % 4
        g = t - e1 - e2

        @pl.when((g >= 0) & (g < 4))
        def _():
            block = quarter * 2 + g // 2
            lanes = pl.ds(pl.multiple_of((g % 2) * 2048, 2048), 2048)
            here = p_buf.at[s, block, :, lanes]
            arrival = p_recv.at[s, quarter * 4 + g]

            @pl.when(e1 + e2 > 0)
            def _():
                remote(here, here, p_trunk.at[s, quarter], arrival, sibling).wait_recv()

            @pl.when((e2 == 0) & (e1 < 3))
            def _():
                remote(here, here, p_trunk.at[s, quarter], arrival, trunk[back]).start()

            @pl.when(e2 < 3)
            def _():
                remote(here, here, p_branch.at[s, quarter], arrival, branch[back]).start()

            pltpu.make_async_copy(here, p_out.at[s, block, :, lanes], out_sem.at[1]).start()

    @pl.loop(0, 12)
    def _(t):
        for way in range(2):
            for s, k in enumerate(panels):
                a_stream(s, k, way, t)
        for quarter in range(4):
            for s, k in enumerate(panels):
                p_stream(s, k, quarter, t)

    for s, k in enumerate(panels):
        x_root, core_root = (k // 2) // 2, (k // 2) % 2
        for way in range(2):
            ahead = (x - x_root + 4) % 4 if way == 0 else (x_root - x + 4) % 4
            half = a_buf.at[s, pl.ds(way * (A_GROUPS // 2), A_GROUPS // 2)]

            @pl.when((core == core_root) & (ahead < 3))
            def _():
                remote(half, half, a_fwd.at[s, way], a_recv.at[s, 0], sibling).wait_send()

            @pl.when(core == core_root)
            def _():
                remote(half, half, a_sib.at[s, way], a_recv.at[s, 0], sibling).wait_send()

        for quarter in range(4):
            back = quarter % 2
            first, second = ((y, k // 4), (z, k % 4)) if quarter < 2 else ((z, k % 4), (y, k // 4))
            e1 = (first[0] - first[1] + 4) % 4 if back == 0 else (first[1] - first[0] + 4) % 4
            e2 = (second[0] - second[1] + 4) % 4 if back == 0 else (second[1] - second[0] + 4) % 4
            part = p_buf.at[s, pl.ds(quarter * 2, 2)]

            @pl.when((e2 == 0) & (e1 < 3))
            def _():
                remote(part, part, p_trunk.at[s, quarter], p_recv.at[s, 0], sibling).wait_send()

            @pl.when(e2 < 3)
            def _():
                remote(part, part, p_branch.at[s, quarter], p_recv.at[s, 0], sibling).wait_send()

    pltpu.make_async_copy(a_buf, a_out, out_sem.at[0]).wait()
    pltpu.make_async_copy(p_buf, p_out, out_sem.at[1]).wait()


def gather_panels(panel, a_blocks, p_blocks):
    anywhere = pl.BlockSpec(memory_space=pl.ANY)
    a_shape = (SECTIONS, A_GROUPS, 16, B * B)
    p_shape = (SECTIONS, P_GROUPS, 16, B * B)
    return pl.pallas_call(
        functools.partial(gather_kernel, panel),
        out_shape=(jax.ShapeDtypeStruct(a_shape, jnp.bfloat16), jax.ShapeDtypeStruct(p_shape, jnp.bfloat16)),
        in_specs=[anywhere] * 2,
        out_specs=(anywhere, anywhere),
        scratch_shapes=[
            pltpu.VMEM(a_shape, jnp.bfloat16),
            pltpu.VMEM(p_shape, jnp.bfloat16),
            pltpu.SemaphoreType.DMA((SECTIONS, A_GROUPS)),
            pltpu.SemaphoreType.DMA((SECTIONS, 16)),
            pltpu.SemaphoreType.DMA((SECTIONS, 2)),
            pltpu.SemaphoreType.DMA((SECTIONS, 2)),
            pltpu.SemaphoreType.DMA((SECTIONS, 4)),
            pltpu.SemaphoreType.DMA((SECTIONS, 4)),
            pltpu.SemaphoreType.DMA((2, SECTIONS)),
            pltpu.SemaphoreType.DMA((2,)),
        ],
        compiler_params=pltpu.CompilerParams(collective_id=1 + panel, has_side_effects=True),
        name=f"gather_{panel}",
    )(a_blocks.reshape(2, A_GROUPS, 16, B * B), p_blocks.reshape(1, P_GROUPS, 16, B * B))


HALF = 512
PART = AGG_DEV * B


def add_rows(total, extra, count):
    @pl.loop(0, count)
    def _(i):
        total[i] = (total[i].astype(jnp.float32) + extra[i].astype(jnp.float32)).astype(jnp.bfloat16)


def reduce_kernel(t_ref, o_ref, own, fwd, in_a, in_b, mid, in2_a, in2_b, local_sem, send, recv, send2, recv2):
    y, z, x, core = place_of()
    y_next = [device((y + 1) % 4, z, x, core), device((y + 3) % 4, z, x, core)]
    z_next = [device(y, (z + 1) % 4, x, core), device(y, (z + 3) % 4, x, core)]
    greet(y_next + z_next)
    here = ((y, z), (z, y))
    nexts = ((y_next, z_next), (z_next, y_next))

    started = []
    for h in range(2):
        u = here[h][0]
        for d in range(2):
            step = (u + 1) % 4 if d == 0 else (u + 3) % 4
            copy = remote(t_ref.at[h, (u + 2) % 4, pl.ds(2 * d, 2)], in_a.at[h, d], send.at[h, d, 0], recv.at[h, d, 0], nexts[h][0][d])
            copy.start()
            started.append(copy)
    for h in range(2):
        u = here[h][0]
        for d in range(2):
            step = (u + 1) % 4 if d == 0 else (u + 3) % 4
            other = 2 * (1 - d)
            copy = remote(t_ref.at[h, step, pl.ds(other, 2)], in_b.at[h, d, pl.ds(other, 2)], send.at[h, d, 1], recv.at[h, d, 1], nexts[h][0][d])
            copy.start()
            started.append(copy)
            pltpu.make_async_copy(t_ref.at[h, step, pl.ds(2 * d, 2)], fwd.at[h, d], local_sem.at[h, d]).start()
        pltpu.make_async_copy(t_ref.at[h, u], own.at[h], local_sem.at[h, 2]).start()

    for h in range(2):
        u = here[h][0]
        for d in range(2):
            step = (u + 1) % 4 if d == 0 else (u + 3) % 4
            pltpu.make_async_copy(t_ref.at[h, step, pl.ds(2 * d, 2)], fwd.at[h, d], local_sem.at[h, d]).wait()
            remote(in_a.at[h, d], in_a.at[h, d], send.at[h, d, 0], recv.at[h, d, 0], nexts[h][0][d]).wait_recv()
            for part in range(2):
                add_rows(fwd.at[h, d, part], in_a.at[h, d, part], 4)
            copy = remote(fwd.at[h, d], in_b.at[h, d, pl.ds(2 * d, 2)], send.at[h, d, 2], recv.at[h, d, 2], nexts[h][0][d])
            copy.start()
            started.append(copy)

    def summed(h, part, i):
        first = own[h, part, i].astype(jnp.float32) + in_b[h, 0, part, i].astype(jnp.float32)
        return first + in_b[h, 1, part, i].astype(jnp.float32)

    for h in range(2):
        u, w = here[h]
        pltpu.make_async_copy(t_ref.at[h, u], own.at[h], local_sem.at[h, 2]).wait()
        for d in range(2):
            other = 2 * (1 - d)
            for part, index in ((other, 1), (2 * d, 2)):
                block = in_b.at[h, d, pl.ds(part, 2)]
                remote(block, block, send.at[h, d, index], recv.at[h, d, index], nexts[h][0][d]).wait_recv()

        opposite = (w + 2) % 4

        @pl.loop(0, 4)
        def _(i):
            mid[h, 2, i] = summed(h, opposite, i).astype(jnp.bfloat16)

        for d in range(2):
            copy = remote(mid.at[h, 2, pl.ds(2 * d, 2)], in2_a.at[h, d], send2.at[h, d, 0], recv2.at[h, d, 0], nexts[h][1][d])
            copy.start()
            started.append(copy)
        for d in range(2):
            step = (w + 1) % 4 if d == 0 else (w + 3) % 4
            other = 2 * (1 - d)

            @pl.loop(0, 2)
            def _(i):
                mid[h, d, other + i] = summed(h, step, other + i).astype(jnp.bfloat16)

            block = pl.ds(other, 2)
            copy = remote(mid.at[h, d, block], in2_b.at[h, d, block], send2.at[h, d, 1], recv2.at[h, d, 1], nexts[h][1][d])
            copy.start()
            started.append(copy)

    for h in range(2):
        u, w = here[h]
        for d in range(2):
            step = (w + 1) % 4 if d == 0 else (w + 3) % 4
            remote(in2_a.at[h, d], in2_a.at[h, d], send2.at[h, d, 0], recv2.at[h, d, 0], nexts[h][1][d]).wait_recv()

            @pl.loop(0, 2)
            def _(i):
                mid[h, d, 2 * d + i] = (summed(h, step, 2 * d + i) + in2_a[h, d, i].astype(jnp.float32)).astype(jnp.bfloat16)

            block = pl.ds(2 * d, 2)
            copy = remote(mid.at[h, d, block], in2_b.at[h, d, block], send2.at[h, d, 2], recv2.at[h, d, 2], nexts[h][1][d])
            copy.start()
            started.append(copy)

    for h in range(2):
        u, w = here[h]
        for d in range(2):
            other = 2 * (1 - d)
            for part, index in ((other, 1), (2 * d, 2)):
                block = in2_b.at[h, d, pl.ds(part, 2)]
                remote(block, block, send2.at[h, d, index], recv2.at[h, d, index], nexts[h][1][d]).wait_recv()

        @pl.loop(0, 4)
        def _(i):
            value = summed(h, w, i) + in2_b[h, 0, i].astype(jnp.float32) + in2_b[h, 1, i].astype(jnp.float32)
            o_ref[pl.ds(pl.multiple_of(i * B, B), B), h * HALF:(h + 1) * HALF] = value

    for copy in started:
        copy.wait_send()


def reduce_terms(term):
    return pl.pallas_call(
        reduce_kernel,
        out_shape=jax.ShapeDtypeStruct((PART, 2 * HALF), jnp.float32),
        in_specs=[pl.BlockSpec(memory_space=pl.ANY)],
        out_specs=pl.BlockSpec(memory_space=pltpu.VMEM),
        scratch_shapes=[
            pltpu.VMEM((2, 4, 4, B, HALF), jnp.bfloat16),
            pltpu.VMEM((2, 2, 2, 4, B, HALF), jnp.bfloat16),
            pltpu.VMEM((2, 2, 2, 4, B, HALF), jnp.bfloat16),
            pltpu.VMEM((2, 2, 4, 4, B, HALF), jnp.bfloat16),
            pltpu.VMEM((2, 3, 4, B, HALF), jnp.bfloat16),
            pltpu.VMEM((2, 2, 2, B, HALF), jnp.bfloat16),
            pltpu.VMEM((2, 2, 4, B, HALF), jnp.bfloat16),
            pltpu.SemaphoreType.DMA((2, 3)),
            pltpu.SemaphoreType.DMA((2, 2, 3)),
            pltpu.SemaphoreType.DMA((2, 2, 3)),
            pltpu.SemaphoreType.DMA((2, 2, 3)),
            pltpu.SemaphoreType.DMA((2, 2, 3)),
        ],
        compiler_params=pltpu.CompilerParams(collective_id=0, has_side_effects=True, vmem_limit_bytes=40 * 1024 * 1024),
        name="reduce_terms",
    )(term)


def halves(x, odd):
    lane = lax.broadcasted_iota(jnp.int32, (x.shape[0], LANES), 1)
    is_odd = jnp.broadcast_to(odd, (x.shape[0], LANES)) == 1
    keep = (lane < 64) != is_odd
    evens, odds = [], []
    for part in range(2):
        own = x[:, part * LANES:(part + 1) * LANES].astype(jnp.float32)
        swapped = pltpu.roll(own, 64, 1)
        evens.append(jnp.where(keep, jnp.where(is_odd, swapped, own), 0.0).astype(jnp.bfloat16))
        odds.append(jnp.where(keep, jnp.where(is_odd, own, swapped), 0.0).astype(jnp.bfloat16))
    return jnp.concatenate(evens, axis=1), jnp.concatenate(odds, axis=1)


def one_hot(position, count):
    rows = lax.broadcasted_iota(jnp.int32, (count, position.shape[1]), 0)
    return jnp.where(rows == position, 1.0, 0.0).astype(jnp.bfloat16)


def dot(a, b):
    return jnp.dot(a, b, preferred_element_type=jnp.float32)


def local_kernel(place, a_ref, p_ref, a_pos, a_odd, p_pos, p_odd, q_ref, mask_ref, out_ref, a_dense, p_rows, p_dense, product, total, staged, out_sem):
    row_index = lax.broadcasted_iota(jnp.int32, (256, 256), 0)
    col_index = lax.broadcasted_iota(jnp.int32, (256, 256), 1)
    swap = jnp.where(col_index == (row_index % 16) * 16 + row_index // 16, 1.0, 0.0).astype(jnp.bfloat16)

    for s in range(SECTIONS):
        p_hot = one_hot(p_pos[s], 128)

        @pl.loop(0, 16)
        def _(q):
            lanes = pl.ds(pl.multiple_of(q * 256, 256), 256)
            parts = halves(p_ref[s, :, lanes], p_odd[s])
            for h in range(2):
                placed = dot(p_hot, parts[h]).astype(jnp.bfloat16)
                for part in range(2):
                    start = pl.multiple_of((q * 4 + part * 2 + h) * KB, KB)
                    for j in range(CB // 2):
                        p_rows[pl.ds(start, KB), j * LANES:(j + 1) * LANES] = placed[j * KB:(j + 1) * KB, part * LANES:(part + 1) * LANES]

        for group in range(4):
            ordered = dot(swap, p_rows[group * 256:(group + 1) * 256, :]).astype(jnp.bfloat16)
            for k in range(KB):
                start = s * KB * B + k * B + group * 16
                p_dense[start:start + 16, :] = ordered[k * 16:(k + 1) * 16, :]

    for s in range(SECTIONS):
        a_hot = one_hot(a_pos[s], 256)

        @pl.loop(0, 16)
        def _(q):
            lanes = pl.ds(pl.multiple_of(q * 256, 256), 256)
            parts = halves(a_ref[s, :, lanes], a_odd[s])
            for h in range(2):
                placed = dot(a_hot, parts[h]).astype(jnp.bfloat16)
                for part in range(2):
                    start = pl.multiple_of((q * 4 + part * 2 + h) * FR, FR)
                    for k in range(KB // 2):
                        lane = s * KB * B + k * LANES
                        a_dense[pl.ds(start, FR), lane:lane + LANES] = placed[k * FR:(k + 1) * FR, part * LANES:(part + 1) * LANES]

    for h in range(2):
        for n in range(2):

            @pl.loop(0, 4)
            def _(m):
                start = pl.multiple_of(m * 512, 512)
                lane = h * HALF + n * 256
                tile = dot(a_dense[pl.ds(start, 512), :], p_dense[:, lane:lane + 256])
                product[2 * n, pl.ds(start, 512), :] = tile[:, :LANES]
                product[2 * n + 1, pl.ds(start, 512), :] = tile[:, LANES:]

        @pl.loop(0, 64)
        def _(g):
            total[g] = jnp.zeros((B, HALF), jnp.float32)

        @pl.loop(0, FR)
        def _(i):
            restrict = q_ref[i]
            lhs = jnp.concatenate([restrict, restrict], axis=1)
            target = place[h, i]
            for j in range(0, 4, 2):
                tops, bottoms = [], []
                for t in (j, j + 1):
                    block = product[t, pl.ds(i, B, stride=FR), :]
                    top = block.astype(jnp.bfloat16)
                    tops.append(top)
                    bottoms.append((block - top.astype(jnp.float32)).astype(jnp.bfloat16))
                rhs = jnp.concatenate([jnp.concatenate(tops, axis=1), jnp.concatenate(bottoms, axis=1)], axis=0)
                term = dot(lhs, rhs).astype(jnp.bfloat16).astype(jnp.float32)
                lanes = slice(j * LANES, (j + 2) * LANES)
                masked = term * mask_ref[i, :, h * HALF + j * LANES:h * HALF + (j + 2) * LANES]
                total[target, :, lanes] += masked

        @pl.loop(0, 64)
        def _(g):
            staged[h, g] = total[g].astype(jnp.bfloat16)

        pltpu.make_async_copy(staged.at[h], out_ref.at[h], out_sem.at[h]).start()

    for h in range(2):
        pltpu.make_async_copy(staged.at[h], out_ref.at[h], out_sem.at[h]).wait()


def local_terms(a, p, a_row, a_col, p_row, p_col, q, place, picked_cols):
    a_pos = ((a_col // 2) * FR + a_row)[:, None, :]
    p_pos = ((p_col // 2) * KB + p_row)[:, None, :]
    a_odd = (a_col % 2)[:, :, None]
    p_odd = (p_col % 2)[:, :, None]
    hit = (picked_cols[:, :, None] == jnp.arange(CB, dtype=jnp.int32)).any(axis=1)
    mask = jnp.repeat(hit.astype(jnp.float32), B, axis=1)[:, None, :]
    q_t = q.reshape(FR, B, B).transpose(0, 2, 1)
    vmem = pl.BlockSpec(memory_space=pltpu.VMEM)
    return pl.pallas_call(
        local_kernel,
        out_shape=jax.ShapeDtypeStruct((2, 64, B, HALF), jnp.bfloat16),
        in_specs=[pl.BlockSpec(memory_space=pltpu.SMEM)] + [vmem] * 8,
        out_specs=pl.BlockSpec(memory_space=pl.ANY),
        scratch_shapes=[
            pltpu.VMEM((FR * B, SECTIONS * KB * B), jnp.bfloat16),
            pltpu.VMEM((KB * B, CB * B), jnp.bfloat16),
            pltpu.VMEM((SECTIONS * KB * B, CB * B), jnp.bfloat16),
            pltpu.VMEM((4, FR * B, LANES), jnp.float32),
            pltpu.VMEM((64, B, HALF), jnp.float32),
            pltpu.VMEM((2, 64, B, HALF), jnp.bfloat16),
            pltpu.SemaphoreType.DMA((2,)),
        ],
        compiler_params=pltpu.CompilerParams(vmem_limit_bytes=60 * 1024 * 1024),
    )(place, a, p, a_pos, a_odd, p_pos, p_odd, q_t, mask)


def per_device(a_blocks, a_row, a_col, p_blocks, p_row, p_col, q_blocks, sched, fine_agg, coarse_place, prod_cols):
    own_row = lax.axis_index("row")
    other = sched[0] + sched[1] - LAST
    a, p = lax.switch(other, [functools.partial(gather_panels, k) for k in range(LAST)], a_blocks, p_blocks)
    order = jnp.stack([jnp.int32(LAST), other])
    row_start = own_row * FR
    picked_cols = lax.dynamic_slice_in_dim(prod_cols, row_start, FR, 0)
    place = coarse_place[lax.dynamic_slice_in_dim(fine_agg, row_start, FR, 0)]
    owner, member = place // AGG_DEV, place % AGG_DEV
    turned = ((owner % 4) * 4 + owner // 4) * AGG_DEV + member
    term = local_terms(
        a.reshape(SECTIONS, FR * 8, B * B),
        p.reshape(SECTIONS, KB * 8, B * B),
        a_row[order],
        a_col[order],
        p_row[order],
        p_col[order],
        q_blocks,
        jnp.stack([place, turned]),
        picked_cols,
    )
    return reduce_terms(term.reshape(2, 4, 4, 4, B, HALF))


def solution(mesh):
    in_specs = (
        P("col", "row", None),
        P(None, "row"),
        P(None, "row"),
        P("row", "col", None),
        P(None, "col"),
        P(None, "col"),
        P("row", None),
        P(),
        P(),
        P(),
        P(None, "col"),
    )
    return jax.shard_map(per_device, mesh=mesh, in_specs=in_specs, out_specs=P("row", "col"), check_vma=False)
```

```python
import functools

import jax
import jax.numpy as jnp
from jax import lax
from jax.experimental import pallas as pl
from jax.experimental.pallas import tpu as pltpu
from jax.sharding import PartitionSpec as P

B = 64
FR = 32
KB = 16
CB = 16
SECTIONS = 2
LANES = 128
AGG_DEV = 4


MESH = pl.DeviceIdType.MESH
LAST = 15
A_GROUPS = 16
P_GROUPS = 8
A_CUT = 1
P_CUT = 4
A_LAG = 2
P_LAG = 3


def remote(src, dst, send_sem, recv_sem, target):
    return pltpu.make_async_remote_copy(
        src_ref=src, dst_ref=dst, send_sem=send_sem, recv_sem=recv_sem, device_id=target, device_id_type=MESH
    )


def greet(targets):
    barrier = pltpu.get_barrier_semaphore()
    for target in targets:
        pl.semaphore_signal(barrier, inc=1, device_id=target, device_id_type=MESH)
    pl.semaphore_wait(barrier, len(targets))


def place_of():
    row, col = lax.axis_index("row"), lax.axis_index("col")
    return row // 4, row % 4, col // 2, col % 2


def device(y, z, x, core):
    return (y * 4 + z, x * 2 + core)


def gather_kernel(panel, a_ref, p_ref, a_out, p_out, a_buf, p_buf, a_recv, p_recv, a_fwd, a_sib, p_trunk, p_branch, load_sem, out_sem):
    y, z, x, core = place_of()
    sibling = device(y, z, x, 1 - core)
    x_next = [device(y, z, (x + 1) % 4, core), device(y, z, (x + 3) % 4, core)]
    y_next = [device((y + 1) % 4, z, x, core), device((y + 3) % 4, z, x, core)]
    z_next = [device(y, (z + 1) % 4, x, core), device(y, (z + 3) % 4, x, core)]
    greet([sibling] + x_next + y_next + z_next)
    panels = (LAST, panel)
    for s, k in enumerate(panels):
        x_root, core_root = (k // 2) // 2, (k // 2) % 2

        @pl.when((x == x_root) & (core == core_root))
        def _():
            pltpu.make_async_copy(a_ref.at[k % 2], a_buf.at[s], load_sem.at[0, s]).start()

        @pl.when((y == k // 4) & (z == k % 4))
        def _():
            pltpu.make_async_copy(p_ref.at[0], p_buf.at[s], load_sem.at[1, s]).start()

    for s, k in enumerate(panels):
        x_root, core_root = (k // 2) // 2, (k // 2) % 2

        @pl.when((x == x_root) & (core == core_root))
        def _():
            pltpu.make_async_copy(a_ref.at[k % 2], a_buf.at[s], load_sem.at[0, s]).wait()

        @pl.when((y == k // 4) & (z == k % 4))
        def _():
            pltpu.make_async_copy(p_ref.at[0], p_buf.at[s], load_sem.at[1, s]).wait()

    def a_stream(s, k, way, t):
        x_root, core_root = (k // 2) // 2, (k // 2) % 2
        ahead = (x - x_root + 4) % 4 if way == 0 else (x_root - x + 4) % 4
        active = core == core_root
        g = t - A_LAG * ahead - jnp.where(active, 0, 1)
        block = way * (A_GROUPS // 2) + g // A_CUT

        @pl.when((g >= 0) & (g < A_GROUPS // 2 * A_CUT))
        def _():
            width = B * B // A_CUT
            lanes = pl.ds(pl.multiple_of((g % A_CUT) * width, width), width)
            here = a_buf.at[s, block, :, lanes]
            arrival = a_recv.at[s, way * (A_GROUPS // 2) * A_CUT + g]

            @pl.when(jnp.logical_not(active & (ahead == 0)))
            def _():
                remote(here, here, a_fwd.at[s, way], arrival, sibling).wait_recv()

            @pl.when(active & (ahead < 3))
            def _():
                remote(here, here, a_fwd.at[s, way], arrival, x_next[way]).start()

            @pl.when(active)
            def _():
                remote(here, here, a_sib.at[s, way], arrival, sibling).start()

            pltpu.make_async_copy(here, a_out.at[s, block, :, lanes], out_sem.at[0]).start()

    def p_stream(s, k, quarter, t):
        back = quarter % 2
        if quarter < 2:
            first, second, trunk, branch = (y, k // 4), (z, k % 4), y_next, z_next
        else:
            first, second, trunk, branch = (z, k % 4), (y, k // 4), z_next, y_next
        e1 = (first[0] - first[1] + 4) % 4 if back == 0 else (first[1] - first[0] + 4) % 4
        e2 = (second[0] - second[1] + 4) % 4 if back == 0 else (second[1] - second[0] + 4) % 4
        g = t - P_LAG * (e1 + e2)

        @pl.when((g >= 0) & (g < 2 * P_CUT))
        def _():
            block = quarter * 2 + g // P_CUT
            width = B * B // P_CUT
            lanes = pl.ds(pl.multiple_of((g % P_CUT) * width, width), width)
            here = p_buf.at[s, block, :, lanes]
            arrival = p_recv.at[s, quarter * 2 * P_CUT + g]

            @pl.when(e1 + e2 > 0)
            def _():
                remote(here, here, p_trunk.at[s, quarter], arrival, sibling).wait_recv()

            @pl.when((e2 == 0) & (e1 < 3))
            def _():
                remote(here, here, p_trunk.at[s, quarter], arrival, trunk[back]).start()

            @pl.when(e2 < 3)
            def _():
                remote(here, here, p_branch.at[s, quarter], arrival, branch[back]).start()

            pltpu.make_async_copy(here, p_out.at[s, block, :, lanes], out_sem.at[1]).start()

    @pl.loop(0, max(A_GROUPS // 2 * A_CUT + 3 * A_LAG + 1, 2 * P_CUT + 6 * P_LAG))
    def _(t):
        for way in range(2):
            for s, k in enumerate(panels):
                a_stream(s, k, way, t)
        for quarter in range(4):
            for s, k in enumerate(panels):
                p_stream(s, k, quarter, t)

    for s, k in enumerate(panels):
        x_root, core_root = (k // 2) // 2, (k // 2) % 2
        for way in range(2):
            ahead = (x - x_root + 4) % 4 if way == 0 else (x_root - x + 4) % 4
            half = a_buf.at[s, pl.ds(way * (A_GROUPS // 2), A_GROUPS // 2)]

            @pl.when((core == core_root) & (ahead < 3))
            def _():
                remote(half, half, a_fwd.at[s, way], a_recv.at[s, 0], sibling).wait_send()

            @pl.when(core == core_root)
            def _():
                remote(half, half, a_sib.at[s, way], a_recv.at[s, 0], sibling).wait_send()

        for quarter in range(4):
            back = quarter % 2
            first, second = ((y, k // 4), (z, k % 4)) if quarter < 2 else ((z, k % 4), (y, k // 4))
            e1 = (first[0] - first[1] + 4) % 4 if back == 0 else (first[1] - first[0] + 4) % 4
            e2 = (second[0] - second[1] + 4) % 4 if back == 0 else (second[1] - second[0] + 4) % 4
            part = p_buf.at[s, pl.ds(quarter * 2, 2)]

            @pl.when((e2 == 0) & (e1 < 3))
            def _():
                remote(part, part, p_trunk.at[s, quarter], p_recv.at[s, 0], sibling).wait_send()

            @pl.when(e2 < 3)
            def _():
                remote(part, part, p_branch.at[s, quarter], p_recv.at[s, 0], sibling).wait_send()

    pltpu.make_async_copy(a_buf, a_out, out_sem.at[0]).wait()
    pltpu.make_async_copy(p_buf, p_out, out_sem.at[1]).wait()


def gather_panels(panel, a_blocks, p_blocks):
    anywhere = pl.BlockSpec(memory_space=pl.ANY)
    a_shape = (SECTIONS, A_GROUPS, 16, B * B)
    p_shape = (SECTIONS, P_GROUPS, 16, B * B)
    return pl.pallas_call(
        functools.partial(gather_kernel, panel),
        out_shape=(jax.ShapeDtypeStruct(a_shape, jnp.bfloat16), jax.ShapeDtypeStruct(p_shape, jnp.bfloat16)),
        in_specs=[anywhere] * 2,
        out_specs=(anywhere, anywhere),
        scratch_shapes=[
            pltpu.VMEM(a_shape, jnp.bfloat16),
            pltpu.VMEM(p_shape, jnp.bfloat16),
            pltpu.SemaphoreType.DMA((SECTIONS, A_GROUPS * A_CUT)),
            pltpu.SemaphoreType.DMA((SECTIONS, P_GROUPS * P_CUT)),
            pltpu.SemaphoreType.DMA((SECTIONS, 2)),
            pltpu.SemaphoreType.DMA((SECTIONS, 2)),
            pltpu.SemaphoreType.DMA((SECTIONS, 4)),
            pltpu.SemaphoreType.DMA((SECTIONS, 4)),
            pltpu.SemaphoreType.DMA((2, SECTIONS)),
            pltpu.SemaphoreType.DMA((2,)),
        ],
        compiler_params=pltpu.CompilerParams(collective_id=1 + panel, has_side_effects=True),
        name=f"gather_{panel}",
    )(a_blocks.reshape(2, A_GROUPS, 16, B * B), p_blocks.reshape(1, P_GROUPS, 16, B * B))


HALF = 512
PART = AGG_DEV * B


def add_rows(total, extra, count):
    @pl.loop(0, count)
    def _(i):
        total[i] = (total[i].astype(jnp.float32) + extra[i].astype(jnp.float32)).astype(jnp.bfloat16)


def reduce_kernel(t_ref, o_ref, own, fwd, in_a, in_b, mid, in2_a, in2_b, local_sem, send, recv, send2, recv2):
    y, z, x, core = place_of()
    y_next = [device((y + 1) % 4, z, x, core), device((y + 3) % 4, z, x, core)]
    z_next = [device(y, (z + 1) % 4, x, core), device(y, (z + 3) % 4, x, core)]
    greet(y_next + z_next)
    here = ((y, z), (z, y))
    nexts = ((y_next, z_next), (z_next, y_next))

    started = []
    for h in range(2):
        u = here[h][0]
        for d in range(2):
            step = (u + 1) % 4 if d == 0 else (u + 3) % 4
            copy = remote(t_ref.at[h, (u + 2) % 4, pl.ds(2 * d, 2)], in_a.at[h, d], send.at[h, d, 0], recv.at[h, d, 0], nexts[h][0][d])
            copy.start()
            started.append(copy)
    for h in range(2):
        u = here[h][0]
        for d in range(2):
            step = (u + 1) % 4 if d == 0 else (u + 3) % 4
            other = 2 * (1 - d)
            copy = remote(t_ref.at[h, step, pl.ds(other, 2)], in_b.at[h, d, pl.ds(other, 2)], send.at[h, d, 1], recv.at[h, d, 1], nexts[h][0][d])
            copy.start()
            started.append(copy)
            pltpu.make_async_copy(t_ref.at[h, step, pl.ds(2 * d, 2)], fwd.at[h, d], local_sem.at[h, d]).start()
        pltpu.make_async_copy(t_ref.at[h, u], own.at[h], local_sem.at[h, 2]).start()

    for h in range(2):
        u = here[h][0]
        for d in range(2):
            step = (u + 1) % 4 if d == 0 else (u + 3) % 4
            pltpu.make_async_copy(t_ref.at[h, step, pl.ds(2 * d, 2)], fwd.at[h, d], local_sem.at[h, d]).wait()
            remote(in_a.at[h, d], in_a.at[h, d], send.at[h, d, 0], recv.at[h, d, 0], nexts[h][0][d]).wait_recv()
            for part in range(2):
                add_rows(fwd.at[h, d, part], in_a.at[h, d, part], 4)
            copy = remote(fwd.at[h, d], in_b.at[h, d, pl.ds(2 * d, 2)], send.at[h, d, 2], recv.at[h, d, 2], nexts[h][0][d])
            copy.start()
            started.append(copy)

    def summed(h, part, i):
        first = own[h, part, i].astype(jnp.float32) + in_b[h, 0, part, i].astype(jnp.float32)
        return first + in_b[h, 1, part, i].astype(jnp.float32)

    for h in range(2):
        u, w = here[h]
        pltpu.make_async_copy(t_ref.at[h, u], own.at[h], local_sem.at[h, 2]).wait()
        for d in range(2):
            other = 2 * (1 - d)
            for part, index in ((other, 1), (2 * d, 2)):
                block = in_b.at[h, d, pl.ds(part, 2)]
                remote(block, block, send.at[h, d, index], recv.at[h, d, index], nexts[h][0][d]).wait_recv()

        opposite = (w + 2) % 4

        @pl.loop(0, 4)
        def _(i):
            mid[h, 2, i] = summed(h, opposite, i).astype(jnp.bfloat16)

        for d in range(2):
            copy = remote(mid.at[h, 2, pl.ds(2 * d, 2)], in2_a.at[h, d], send2.at[h, d, 0], recv2.at[h, d, 0], nexts[h][1][d])
            copy.start()
            started.append(copy)
        for d in range(2):
            step = (w + 1) % 4 if d == 0 else (w + 3) % 4
            other = 2 * (1 - d)

            @pl.loop(0, 2)
            def _(i):
                mid[h, d, other + i] = summed(h, step, other + i).astype(jnp.bfloat16)

            block = pl.ds(other, 2)
            copy = remote(mid.at[h, d, block], in2_b.at[h, d, block], send2.at[h, d, 1], recv2.at[h, d, 1], nexts[h][1][d])
            copy.start()
            started.append(copy)

    for h in range(2):
        u, w = here[h]
        for d in range(2):
            step = (w + 1) % 4 if d == 0 else (w + 3) % 4
            remote(in2_a.at[h, d], in2_a.at[h, d], send2.at[h, d, 0], recv2.at[h, d, 0], nexts[h][1][d]).wait_recv()

            @pl.loop(0, 2)
            def _(i):
                mid[h, d, 2 * d + i] = (summed(h, step, 2 * d + i) + in2_a[h, d, i].astype(jnp.float32)).astype(jnp.bfloat16)

            block = pl.ds(2 * d, 2)
            copy = remote(mid.at[h, d, block], in2_b.at[h, d, block], send2.at[h, d, 2], recv2.at[h, d, 2], nexts[h][1][d])
            copy.start()
            started.append(copy)

    for h in range(2):
        u, w = here[h]
        for d in range(2):
            other = 2 * (1 - d)
            for part, index in ((other, 1), (2 * d, 2)):
                block = in2_b.at[h, d, pl.ds(part, 2)]
                remote(block, block, send2.at[h, d, index], recv2.at[h, d, index], nexts[h][1][d]).wait_recv()

        @pl.loop(0, 4)
        def _(i):
            value = summed(h, w, i) + in2_b[h, 0, i].astype(jnp.float32) + in2_b[h, 1, i].astype(jnp.float32)
            o_ref[pl.ds(pl.multiple_of(i * B, B), B), h * HALF:(h + 1) * HALF] = value

    for copy in started:
        copy.wait_send()


def reduce_terms(term):
    return pl.pallas_call(
        reduce_kernel,
        out_shape=jax.ShapeDtypeStruct((PART, 2 * HALF), jnp.float32),
        in_specs=[pl.BlockSpec(memory_space=pl.ANY)],
        out_specs=pl.BlockSpec(memory_space=pltpu.VMEM),
        scratch_shapes=[
            pltpu.VMEM((2, 4, 4, B, HALF), jnp.bfloat16),
            pltpu.VMEM((2, 2, 2, 4, B, HALF), jnp.bfloat16),
            pltpu.VMEM((2, 2, 2, 4, B, HALF), jnp.bfloat16),
            pltpu.VMEM((2, 2, 4, 4, B, HALF), jnp.bfloat16),
            pltpu.VMEM((2, 3, 4, B, HALF), jnp.bfloat16),
            pltpu.VMEM((2, 2, 2, B, HALF), jnp.bfloat16),
            pltpu.VMEM((2, 2, 4, B, HALF), jnp.bfloat16),
            pltpu.SemaphoreType.DMA((2, 3)),
            pltpu.SemaphoreType.DMA((2, 2, 3)),
            pltpu.SemaphoreType.DMA((2, 2, 3)),
            pltpu.SemaphoreType.DMA((2, 2, 3)),
            pltpu.SemaphoreType.DMA((2, 2, 3)),
        ],
        compiler_params=pltpu.CompilerParams(collective_id=0, has_side_effects=True, vmem_limit_bytes=62 * 1024 * 1024),
        name="reduce_terms",
    )(term)


def halves(x, is_odd, keep):
    evens, odds = [], []
    for part in range(2):
        own = x[:, part * LANES:(part + 1) * LANES].astype(jnp.float32)
        swapped = pltpu.roll(own, 64, 1)
        evens.append(jnp.where(keep, jnp.where(is_odd, swapped, own), 0.0).astype(jnp.bfloat16))
        odds.append(jnp.where(keep, jnp.where(is_odd, own, swapped), 0.0).astype(jnp.bfloat16))
    return jnp.concatenate(evens, axis=1), jnp.concatenate(odds, axis=1)


def one_hot(position, count):
    rows = lax.broadcasted_iota(jnp.int32, (count, position.shape[1]), 0)
    return jnp.where(rows == position, 1.0, 0.0).astype(jnp.bfloat16)


def parity(cols):
    odd = (cols % 2).astype(jnp.float32)
    is_odd = jnp.broadcast_to(odd, (LANES, cols.shape[1])).T > 0.5
    lane = lax.broadcasted_iota(jnp.int32, is_odd.shape, 1)
    return is_odd, (lane < 64) != is_odd


def dot(a, b):
    return jnp.dot(a, b, preferred_element_type=jnp.float32)


UN_Q = 2
UN_I = 4


def local_kernel(sched, fine_agg, coarse_place, a_ref, p_ref, a_row, a_col, p_row, p_col, q_ref, cols_ref, out_ref,
                 a_dense, p_rows, p_dense, product, total, staged, mask, q_rows, out_sem):
    own_row = lax.axis_index("row")
    row_index = lax.broadcasted_iota(jnp.int32, (256, 256), 0)
    col_index = lax.broadcasted_iota(jnp.int32, (256, 256), 1)
    swap = jnp.where(col_index == (row_index % 16) * 16 + row_index // 16, 1.0, 0.0).astype(jnp.bfloat16)
    panels = (LAST, sched[0] + sched[1] - LAST)

    a_hot, a_par, p_hot, p_par = [], [], [], []
    for k in panels:
        pick = pl.ds(k, 1)
        a_hot.append(one_hot((a_col[pick, :] // 2) * FR + a_row[pick, :], 256))
        p_hot.append(one_hot((p_col[pick, :] // 2) * KB + p_row[pick, :], 128))
        a_par.append(parity(a_col[pick, :]))
        p_par.append(parity(p_col[pick, :]))

    block_of = lax.broadcasted_iota(jnp.int32, (FR, CB * B), 1) // B
    picked = cols_ref[pl.ds(pl.multiple_of(own_row * FR, FR), FR), :]
    hit = block_of == picked[:, 0:1]
    for n in range(1, picked.shape[1]):
        hit = hit | (block_of == picked[:, n:n + 1])
    mask[...] = jnp.where(hit, 1.0, 0.0)
    for r in range(FR):
        q_rows[r * FR:(r + 1) * FR, :] = q_ref[:, r * LANES:(r + 1) * LANES].astype(jnp.float32)

    @pl.loop(0, 16, unroll=UN_Q)
    def _(q):
        lanes = pl.ds(pl.multiple_of(q * 256, 256), 256)
        for s in range(SECTIONS):
            parts = halves(p_ref[s, :, lanes], *p_par[s])
            for h in range(2):
                placed = dot(p_hot[s], parts[h]).astype(jnp.bfloat16)
                for part in range(2):
                    start = pl.multiple_of((q * 4 + part * 2 + h) * KB, KB)
                    for j in range(CB // 2):
                        p_rows[s, pl.ds(start, KB), j * LANES:(j + 1) * LANES] = placed[j * KB:(j + 1) * KB, part * LANES:(part + 1) * LANES]
            parts = halves(a_ref[s, :, lanes], *a_par[s])
            for h in range(2):
                placed = dot(a_hot[s], parts[h]).astype(jnp.bfloat16)
                for part in range(2):
                    start = pl.multiple_of((h * (B // 2) + q * 2 + part) * FR, FR)
                    for k in range(KB // 2):
                        lane = s * KB * B + k * LANES
                        a_dense[pl.ds(start, FR), lane:lane + LANES] = placed[k * FR:(k + 1) * FR, part * LANES:(part + 1) * LANES]

    for s in range(SECTIONS):
        for group in range(4):
            ordered = dot(swap, p_rows[s, group * 256:(group + 1) * 256, :]).astype(jnp.bfloat16)
            for k in range(KB):
                start = s * KB * B + k * B + group * 16
                p_dense[start:start + 16, :] = ordered[k * 16:(k + 1) * 16, :]

    for h in range(2):
        for n in range(2):

            @pl.loop(0, 4)
            def _(m):
                start = pl.multiple_of(m * 512, 512)
                lane = h * HALF + n * 256
                tile = dot(a_dense[pl.ds(start, 512), :], p_dense[:, lane:lane + 256])
                product[2 * n, pl.ds(start, 512), :] = tile[:, :LANES]
                product[2 * n + 1, pl.ds(start, 512), :] = tile[:, LANES:]

        @pl.loop(0, 64)
        def _(g):
            total[g] = jnp.zeros((B, HALF), jnp.float32)

        @pl.loop(0, FR, step=UN_I)
        def _(first):
            terms = []
            for u in range(UN_I):
                i = first + u
                pair = q_rows[pl.ds(i, B // 2, stride=FR), :]
                flipped = jnp.concatenate([pair, pltpu.roll(pair, 64, 1)], axis=0)[:, :B]
                lhs = jnp.concatenate([flipped, flipped], axis=0).astype(jnp.bfloat16)
                for j in range(0, 4, 2):
                    tops, bottoms = [], []
                    for t in (j, j + 1):
                        block = product[t, pl.ds(i, B, stride=FR), :]
                        top = block.astype(jnp.bfloat16)
                        tops.append(top)
                        bottoms.append((block - top.astype(jnp.float32)).astype(jnp.bfloat16))
                    rhs = jnp.concatenate([jnp.concatenate(tops, axis=1), jnp.concatenate(bottoms, axis=1)], axis=0)
                    term = lax.dot_general(lhs, rhs, (((0,), (0,)), ((), ())), preferred_element_type=jnp.float32)
                    terms.append(term.astype(jnp.bfloat16).astype(jnp.float32))
            for u in range(UN_I):
                i = first + u
                place = coarse_place[fine_agg[own_row * FR + i]]
                owner, member = place // AGG_DEV, place % AGG_DEV
                target = place if h == 0 else ((owner % 4) * 4 + owner // 4) * AGG_DEV + member
                for j in range(0, 4, 2):
                    lanes = slice(j * LANES, (j + 2) * LANES)
                    keep = mask[pl.ds(i, 1), h * HALF + j * LANES:h * HALF + (j + 2) * LANES]
                    total[target, :, lanes] += terms[u * 2 + j // 2] * keep

        @pl.loop(0, 64)
        def _(g):
            staged[h, g] = total[g].astype(jnp.bfloat16)

        pltpu.make_async_copy(staged.at[h], out_ref.at[h], out_sem.at[h]).start()

    for h in range(2):
        pltpu.make_async_copy(staged.at[h], out_ref.at[h], out_sem.at[h]).wait()


def local_terms(sched, fine_agg, coarse_place, a, p, a_row, a_col, p_row, p_col, q, prod_cols):
    smem = pl.BlockSpec(memory_space=pltpu.SMEM)
    vmem = pl.BlockSpec(memory_space=pltpu.VMEM)
    return pl.pallas_call(
        local_kernel,
        out_shape=jax.ShapeDtypeStruct((2, 64, B, HALF), jnp.bfloat16),
        in_specs=[smem] * 3 + [vmem] * 8,
        out_specs=pl.BlockSpec(memory_space=pl.ANY),
        scratch_shapes=[
            pltpu.VMEM((FR * B, SECTIONS * KB * B), jnp.bfloat16),
            pltpu.VMEM((SECTIONS, KB * B, CB * B), jnp.bfloat16),
            pltpu.VMEM((SECTIONS * KB * B, CB * B), jnp.bfloat16),
            pltpu.VMEM((4, FR * B, LANES), jnp.float32),
            pltpu.VMEM((64, B, HALF), jnp.float32),
            pltpu.VMEM((2, 64, B, HALF), jnp.bfloat16),
            pltpu.VMEM((FR, CB * B), jnp.float32),
            pltpu.VMEM((FR * B // 2, LANES), jnp.float32),
            pltpu.SemaphoreType.DMA((2,)),
        ],
        compiler_params=pltpu.CompilerParams(vmem_limit_bytes=60 * 1024 * 1024),
        name="local_terms",
    )(sched, fine_agg, coarse_place, a, p, a_row, a_col, p_row, p_col, q, prod_cols)


def per_device(a_blocks, a_row, a_col, p_blocks, p_row, p_col, q_blocks, sched, fine_agg, coarse_place, prod_cols):
    other = sched[0] + sched[1] - LAST
    a, p = lax.switch(other, [functools.partial(gather_panels, k) for k in range(LAST)], a_blocks, p_blocks)
    term = local_terms(
        sched,
        fine_agg,
        coarse_place,
        a.reshape(SECTIONS, FR * 8, B * B),
        p.reshape(SECTIONS, KB * 8, B * B),
        a_row,
        a_col,
        p_row,
        p_col,
        q_blocks,
        prod_cols,
    )
    return reduce_terms(term.reshape(2, 4, 4, 4, B, HALF))


def solution(mesh):
    in_specs = (
        P("col", "row", None),
        P(None, "row"),
        P(None, "row"),
        P("row", "col", None),
        P(None, "col"),
        P(None, "col"),
        P("row", None),
        P(),
        P(),
        P(),
        P(None, "col"),
    )
    return jax.shard_map(per_device, mesh=mesh, in_specs=in_specs, out_specs=P("row", "col"), check_vma=False)
```

```python
import functools

import jax
import jax.numpy as jnp
from jax import lax
from jax.experimental import pallas as pl
from jax.experimental.pallas import tpu as pltpu
from jax.sharding import PartitionSpec as P

B = 64
FR = 32
KB = 16
CB = 16
SECTIONS = 2
LANES = 128
AGG_DEV = 4


MESH = pl.DeviceIdType.MESH
LAST = 15
A_GROUPS = 16
P_GROUPS = 8
A_CUT = 1
A_LAG = 2
P_TIMES = (5, 7, 8, 10, 13)


def remote(src, dst, send_sem, recv_sem, target):
    return pltpu.make_async_remote_copy(
        src_ref=src, dst_ref=dst, send_sem=send_sem, recv_sem=recv_sem, device_id=target, device_id_type=MESH
    )


def greet(targets, distant=()):
    barrier = pltpu.get_barrier_semaphore()
    everyone = list(distant) + list(targets)
    for target in everyone:
        pl.semaphore_signal(barrier, inc=1, device_id=target, device_id_type=MESH)
    pl.semaphore_wait(barrier, len(everyone))


def place_of():
    row, col = lax.axis_index("row"), lax.axis_index("col")
    return row // 4, row % 4, col // 2, col % 2


def device(y, z, x, core):
    return (y * 4 + z, x * 2 + core)


def gather_kernel(panel, a_ref, p_ref, a_out, p_out, a_buf, p_buf, a_recv, a_fwd, a_sib, line_send, line_recv, across_send, across_recv,
                  far_send, far_recv, along_send, along_recv, relay_send, relay_recv, load_sem, out_sem):
    y, z, x, core = place_of()
    sibling = device(y, z, x, 1 - core)
    x_next = [device(y, z, (x + 1) % 4, core), device(y, z, (x + 3) % 4, core)]
    y_next = [device((y + 1) % 4, z, x, core), device((y + 3) % 4, z, x, core)]
    z_next = [device(y, (z + 1) % 4, x, core), device(y, (z + 3) % 4, x, core)]
    panels = (LAST, panel)
    chunks = A_GROUPS // 2 * A_CUT
    width = B * B // A_CUT
    parts = [pl.ds(0, B * B // 2), pl.ds(B * B // 2, B * B // 2)]

    for s, k in enumerate(panels):
        @pl.when((x == (k // 2) // 2) & (core == (k // 2) % 2))
        def _():
            pltpu.make_async_copy(a_ref.at[k % 2], a_buf.at[s], load_sem.at[0, s]).start()

        @pl.when((y == k // 4) & (z == k % 4))
        def _():
            pltpu.make_async_copy(p_ref.at[0], p_buf.at[s], load_sem.at[1, s]).start()

    greet([sibling] + x_next + y_next + z_next, [device((y + 2) % 4, z, x, core), device(y, (z + 2) % 4, x, core)])

    for s, k in enumerate(panels):
        @pl.when((y == k // 4) & (z == k % 4))
        def _():
            pltpu.make_async_copy(p_ref.at[0], p_buf.at[s], load_sem.at[1, s]).wait()

        @pl.when((x == (k // 2) // 2) & (core == (k // 2) % 2))
        def _():
            pltpu.make_async_copy(a_ref.at[k % 2], a_buf.at[s], load_sem.at[0, s]).wait()

    def a_role(k, way):
        x_root, core_root = (k // 2) // 2, (k // 2) % 2
        ahead = (x - x_root + 4) % 4 if way == 0 else (x_root - x + 4) % 4
        active = core == way
        origin = (ahead == 0) & (core == core_root)
        onward = active & (ahead < 3)
        if core_root == way:
            return ahead, origin, onward, active, A_LAG * ahead + jnp.where(active, 0, 1)
        lag = jnp.where(origin, 0, A_LAG * ahead + jnp.where(active, 1, 2))
        return ahead, origin, onward, (active & (ahead > 0)) | origin, lag

    def a_stream(s, k, way, t):
        ahead, origin, onward, sideways, lag = a_role(k, way)
        g = t - lag

        @pl.when((g >= 0) & (g < chunks))
        def _():
            block = way * (A_GROUPS // 2) + g // A_CUT
            lanes = pl.ds(pl.multiple_of((g % A_CUT) * width, width), width)
            here = a_buf.at[s, block, :, lanes]
            arrival = a_recv.at[s, way * chunks + g]

            @pl.when(jnp.logical_not(origin))
            def _():
                remote(here, here, a_fwd.at[s, way], arrival, sibling).wait_recv()

            @pl.when(onward)
            def _():
                remote(here, here, a_fwd.at[s, way], arrival, x_next[way]).start()

            @pl.when(sideways)
            def _():
                remote(here, here, a_sib.at[s, way], arrival, sibling).start()

            pltpu.make_async_copy(here, a_out.at[s, block, :, lanes], out_sem.at[0]).start()

    def p_role(k, f):
        if f == 0:
            u, w, u_root, w_root, u_next, w_next = y, z, k // 4, k % 4, y_next, z_next
        else:
            u, w, u_root, w_root, u_next, w_next = z, y, k % 4, k // 4, z_next, y_next
        du, dw = (u - u_root + 4) % 4, (w - w_root + 4) % 4
        clear = [jnp.logical_not((dw == 0) & (du == 3)), jnp.logical_not((dw == 0) & (du == 1))]
        return u, u_root, w_root, u_next, w_next, du, dw, clear

    pairs = [(s, k, f) for s, k in enumerate(panels) for f in range(2)]

    def along(s, f, u, u_next, clear):
        group = p_buf.at[s, f * 4 + u]
        for d in range(2):
            @pl.when(clear[d])
            def _():
                remote(group, group, along_send.at[s, f, d], along_recv.at[s, f, d], u_next[d]).start()

    def relay(s, f, u, u_next, clear, d):
        group = p_buf.at[s, f * 4 + (u + (3 if d == 0 else 1)) % 4, :, parts[d]]

        @pl.when(clear[d])
        def _():
            remote(group, group, relay_send.at[s, f, d], relay_recv.at[s, f, d], u_next[d]).start()

    def across(s, f, u, w_next):
        group = p_buf.at[s, f * 4 + u]
        for d in range(2):
            remote(group, group, across_send.at[s, f, d], across_recv.at[s, f, d], w_next[d]).start()

    for s, k, f in pairs:
        u, u_root, w_root, u_next, w_next, du, dw, clear = p_role(k, f)

        @pl.when((du == 0) & (dw == 0))
        def _():
            for j in (2, 1, 3):
                g = (u_root + j) % 4
                group = p_buf.at[s, f * 4 + g]
                target = device(g, w_root, x, core) if f == 0 else device(w_root, g, x, core)
                remote(group, group, line_send.at[s, f, j - 1], line_recv.at[s, f], target).start()
            across(s, f, u, w_next)
            along(s, f, u, u_next, clear)
            for d in range(2):
                relay(s, f, u, u_next, clear, d)

    def first_arrivals():
        for s, k, f in pairs:
            u, u_root, w_root, u_next, w_next, du, dw, clear = p_role(k, f)

            @pl.when((du != 0) & (dw == 0))
            def _():
                group = p_buf.at[s, f * 4 + u]
                remote(group, group, line_send.at[s, f, 0], line_recv.at[s, f], sibling).wait_recv()
                across(s, f, u, w_next)
                along(s, f, u, u_next, clear)

    def second_arrivals():
        for s, k, f in pairs:
            u, u_root, w_root, u_next, w_next, du, dw, clear = p_role(k, f)
            for d in range(2):
                @pl.when(dw == (1 if d == 0 else 3))
                def _():
                    group = p_buf.at[s, f * 4 + u]
                    remote(group, group, across_send.at[s, f, d], across_recv.at[s, f, d], sibling).wait_recv()
                    half = p_buf.at[s, f * 4 + u, :, parts[d]]
                    remote(half, half, far_send.at[s, f, d], far_recv.at[s, f, d], w_next[d]).start()
                    along(s, f, u, u_next, clear)

    def third_arrivals():
        for s, k, f in pairs:
            u, u_root, w_root, u_next, w_next, du, dw, clear = p_role(k, f)

            @pl.when(dw == 2)
            def _():
                for d in range(2):
                    half = p_buf.at[s, f * 4 + u, :, parts[d]]
                    remote(half, half, far_send.at[s, f, d], far_recv.at[s, f, d], sibling).wait_recv()
                along(s, f, u, u_next, clear)

    def fourth_arrivals():
        for s, k, f in pairs:
            u, u_root, w_root, u_next, w_next, du, dw, clear = p_role(k, f)

            @pl.when((du != 0) | (dw != 0))
            def _():
                for d in range(2):
                    group = p_buf.at[s, f * 4 + (u + (3 if d == 0 else 1)) % 4]
                    remote(group, group, along_send.at[s, f, d], along_recv.at[s, f, d], sibling).wait_recv()
                    relay(s, f, u, u_next, clear, d)

    def last_arrivals():
        for s, k, f in pairs:
            u, u_root, w_root, u_next, w_next, du, dw, clear = p_role(k, f)

            @pl.when((du != 0) | (dw != 0))
            def _():
                for d in range(2):
                    group = p_buf.at[s, f * 4 + (u + 2) % 4, :, parts[d]]
                    remote(group, group, relay_send.at[s, f, d], relay_recv.at[s, f, d], sibling).wait_recv()

        pltpu.make_async_copy(p_buf, p_out, out_sem.at[1]).start()

    @pl.loop(0, chunks + 3 * A_LAG + 2)
    def _(t):
        for s, k in enumerate(panels):
            for way in range(2):
                a_stream(s, k, way, t)
        for when, act in zip(P_TIMES, (first_arrivals, second_arrivals, third_arrivals, fourth_arrivals, last_arrivals)):
            pl.when(t == when)(act)

    for s, k in enumerate(panels):
        for way in range(2):
            ahead, origin, onward, sideways, lag = a_role(k, way)
            half = a_buf.at[s, pl.ds(way * (A_GROUPS // 2), A_GROUPS // 2)]

            @pl.when(onward)
            def _():
                remote(half, half, a_fwd.at[s, way], a_recv.at[s, 0], sibling).wait_send()

            @pl.when(sideways)
            def _():
                remote(half, half, a_sib.at[s, way], a_recv.at[s, 0], sibling).wait_send()

    for s, k, f in pairs:
        u, u_root, w_root, u_next, w_next, du, dw, clear = p_role(k, f)
        group = p_buf.at[s, f * 4 + u]
        half = p_buf.at[s, f * 4 + u, :, parts[0]]

        @pl.when((du == 0) & (dw == 0))
        def _():
            for j in range(3):
                remote(group, group, line_send.at[s, f, j], line_recv.at[s, f], sibling).wait_send()

        for d in range(2):
            @pl.when(dw == 0)
            def _():
                remote(group, group, across_send.at[s, f, d], across_recv.at[s, f, d], sibling).wait_send()

            @pl.when(dw == (1 if d == 0 else 3))
            def _():
                remote(half, half, far_send.at[s, f, d], far_recv.at[s, f, d], sibling).wait_send()

            @pl.when(clear[d])
            def _():
                remote(group, group, along_send.at[s, f, d], along_recv.at[s, f, d], sibling).wait_send()
                remote(half, half, relay_send.at[s, f, d], relay_recv.at[s, f, d], sibling).wait_send()

    pltpu.make_async_copy(a_buf, a_out, out_sem.at[0]).wait()
    pltpu.make_async_copy(p_buf, p_out, out_sem.at[1]).wait()


def gather_panels(panel, a_blocks, p_blocks):
    anywhere = pl.BlockSpec(memory_space=pl.ANY)
    a_shape = (SECTIONS, A_GROUPS, 16, B * B)
    p_shape = (SECTIONS, P_GROUPS, 16, B * B)
    dma = pltpu.SemaphoreType.DMA
    ends = [dma((SECTIONS, 2, 2)), dma((SECTIONS, 2, 2))]
    return pl.pallas_call(
        functools.partial(gather_kernel, panel),
        out_shape=(jax.ShapeDtypeStruct(a_shape, jnp.bfloat16), jax.ShapeDtypeStruct(p_shape, jnp.bfloat16)),
        in_specs=[anywhere] * 2,
        out_specs=(anywhere, anywhere),
        scratch_shapes=[
            pltpu.VMEM(a_shape, jnp.bfloat16),
            pltpu.VMEM(p_shape, jnp.bfloat16),
            dma((SECTIONS, A_GROUPS * A_CUT)),
            dma((SECTIONS, 2)),
            dma((SECTIONS, 2)),
            dma((SECTIONS, 2, 3)),
            dma((SECTIONS, 2)),
        ]
        + ends * 4
        + [dma((2, SECTIONS)), dma((2,))],
        compiler_params=pltpu.CompilerParams(collective_id=1 + panel, has_side_effects=True),
        name=f"gather_{panel}",
    )(a_blocks.reshape(2, A_GROUPS, 16, B * B), p_blocks.reshape(1, P_GROUPS, 16, B * B))


HALF = 512
PART = AGG_DEV * B


def add_rows(total, extra, count):
    @pl.loop(0, count)
    def _(i):
        total[i] = (total[i].astype(jnp.float32) + extra[i].astype(jnp.float32)).astype(jnp.bfloat16)


def reduce_kernel(t_ref, o_ref, own, fwd, in_a, in_b, mid, in2_a, in2_b, local_sem, send, recv, send2, recv2):
    y, z, x, core = place_of()
    y_next = [device((y + 1) % 4, z, x, core), device((y + 3) % 4, z, x, core)]
    z_next = [device(y, (z + 1) % 4, x, core), device(y, (z + 3) % 4, x, core)]
    greet(y_next + z_next)
    here = ((y, z), (z, y))
    nexts = ((y_next, z_next), (z_next, y_next))

    started = []
    for h in range(2):
        u = here[h][0]
        for d in range(2):
            step = (u + 1) % 4 if d == 0 else (u + 3) % 4
            copy = remote(t_ref.at[h, (u + 2) % 4, pl.ds(2 * d, 2)], in_a.at[h, d], send.at[h, d, 0], recv.at[h, d, 0], nexts[h][0][d])
            copy.start()
            started.append(copy)
    for h in range(2):
        u = here[h][0]
        for d in range(2):
            step = (u + 1) % 4 if d == 0 else (u + 3) % 4
            other = 2 * (1 - d)
            copy = remote(t_ref.at[h, step, pl.ds(other, 2)], in_b.at[h, d, pl.ds(other, 2)], send.at[h, d, 1], recv.at[h, d, 1], nexts[h][0][d])
            copy.start()
            started.append(copy)
            pltpu.make_async_copy(t_ref.at[h, step, pl.ds(2 * d, 2)], fwd.at[h, d], local_sem.at[h, d]).start()
        pltpu.make_async_copy(t_ref.at[h, u], own.at[h], local_sem.at[h, 2]).start()

    for h in range(2):
        u = here[h][0]
        for d in range(2):
            step = (u + 1) % 4 if d == 0 else (u + 3) % 4
            pltpu.make_async_copy(t_ref.at[h, step, pl.ds(2 * d, 2)], fwd.at[h, d], local_sem.at[h, d]).wait()
            remote(in_a.at[h, d], in_a.at[h, d], send.at[h, d, 0], recv.at[h, d, 0], nexts[h][0][d]).wait_recv()
            for part in range(2):
                add_rows(fwd.at[h, d, part], in_a.at[h, d, part], 4)
            copy = remote(fwd.at[h, d], in_b.at[h, d, pl.ds(2 * d, 2)], send.at[h, d, 2], recv.at[h, d, 2], nexts[h][0][d])
            copy.start()
            started.append(copy)

    def summed(h, part, i):
        first = own[h, part, i].astype(jnp.float32) + in_b[h, 0, part, i].astype(jnp.float32)
        return first + in_b[h, 1, part, i].astype(jnp.float32)

    for h in range(2):
        u, w = here[h]
        pltpu.make_async_copy(t_ref.at[h, u], own.at[h], local_sem.at[h, 2]).wait()
        for d in range(2):
            other = 2 * (1 - d)
            for part, index in ((other, 1), (2 * d, 2)):
                block = in_b.at[h, d, pl.ds(part, 2)]
                remote(block, block, send.at[h, d, index], recv.at[h, d, index], nexts[h][0][d]).wait_recv()

        opposite = (w + 2) % 4

        @pl.loop(0, 4)
        def _(i):
            mid[h, 2, i] = summed(h, opposite, i).astype(jnp.bfloat16)

        for d in range(2):
            copy = remote(mid.at[h, 2, pl.ds(2 * d, 2)], in2_a.at[h, d], send2.at[h, d, 0], recv2.at[h, d, 0], nexts[h][1][d])
            copy.start()
            started.append(copy)
        for d in range(2):
            step = (w + 1) % 4 if d == 0 else (w + 3) % 4
            other = 2 * (1 - d)

            @pl.loop(0, 2)
            def _(i):
                mid[h, d, other + i] = summed(h, step, other + i).astype(jnp.bfloat16)

            block = pl.ds(other, 2)
            copy = remote(mid.at[h, d, block], in2_b.at[h, d, block], send2.at[h, d, 1], recv2.at[h, d, 1], nexts[h][1][d])
            copy.start()
            started.append(copy)

    for h in range(2):
        u, w = here[h]
        for d in range(2):
            step = (w + 1) % 4 if d == 0 else (w + 3) % 4
            remote(in2_a.at[h, d], in2_a.at[h, d], send2.at[h, d, 0], recv2.at[h, d, 0], nexts[h][1][d]).wait_recv()

            @pl.loop(0, 2)
            def _(i):
                mid[h, d, 2 * d + i] = (summed(h, step, 2 * d + i) + in2_a[h, d, i].astype(jnp.float32)).astype(jnp.bfloat16)

            block = pl.ds(2 * d, 2)
            copy = remote(mid.at[h, d, block], in2_b.at[h, d, block], send2.at[h, d, 2], recv2.at[h, d, 2], nexts[h][1][d])
            copy.start()
            started.append(copy)

    for h in range(2):
        u, w = here[h]
        for d in range(2):
            other = 2 * (1 - d)
            for part, index in ((other, 1), (2 * d, 2)):
                block = in2_b.at[h, d, pl.ds(part, 2)]
                remote(block, block, send2.at[h, d, index], recv2.at[h, d, index], nexts[h][1][d]).wait_recv()

        @pl.loop(0, 4)
        def _(i):
            value = summed(h, w, i) + in2_b[h, 0, i].astype(jnp.float32) + in2_b[h, 1, i].astype(jnp.float32)
            o_ref[pl.ds(pl.multiple_of(i * B, B), B), h * HALF:(h + 1) * HALF] = value

    for copy in started:
        copy.wait_send()


def reduce_terms(term):
    return pl.pallas_call(
        reduce_kernel,
        out_shape=jax.ShapeDtypeStruct((PART, 2 * HALF), jnp.float32),
        in_specs=[pl.BlockSpec(memory_space=pl.ANY)],
        out_specs=pl.BlockSpec(memory_space=pltpu.VMEM),
        scratch_shapes=[
            pltpu.VMEM((2, 4, 4, B, HALF), jnp.bfloat16),
            pltpu.VMEM((2, 2, 2, 4, B, HALF), jnp.bfloat16),
            pltpu.VMEM((2, 2, 2, 4, B, HALF), jnp.bfloat16),
            pltpu.VMEM((2, 2, 4, 4, B, HALF), jnp.bfloat16),
            pltpu.VMEM((2, 3, 4, B, HALF), jnp.bfloat16),
            pltpu.VMEM((2, 2, 2, B, HALF), jnp.bfloat16),
            pltpu.VMEM((2, 2, 4, B, HALF), jnp.bfloat16),
            pltpu.SemaphoreType.DMA((2, 3)),
            pltpu.SemaphoreType.DMA((2, 2, 3)),
            pltpu.SemaphoreType.DMA((2, 2, 3)),
            pltpu.SemaphoreType.DMA((2, 2, 3)),
            pltpu.SemaphoreType.DMA((2, 2, 3)),
        ],
        compiler_params=pltpu.CompilerParams(collective_id=0, has_side_effects=True, vmem_limit_bytes=62 * 1024 * 1024),
        name="reduce_terms",
    )(term)


def halves(x, is_odd, keep):
    evens, odds = [], []
    for part in range(2):
        own = x[:, part * LANES:(part + 1) * LANES].astype(jnp.float32)
        swapped = pltpu.roll(own, 64, 1)
        evens.append(jnp.where(keep, jnp.where(is_odd, swapped, own), 0.0).astype(jnp.bfloat16))
        odds.append(jnp.where(keep, jnp.where(is_odd, own, swapped), 0.0).astype(jnp.bfloat16))
    return jnp.concatenate(evens, axis=1), jnp.concatenate(odds, axis=1)


def one_hot(position, count):
    rows = lax.broadcasted_iota(jnp.int32, (count, position.shape[1]), 0)
    return jnp.where(rows == position, 1.0, 0.0).astype(jnp.bfloat16)


def parity(cols):
    odd = (cols % 2).astype(jnp.float32)
    is_odd = jnp.broadcast_to(odd, (LANES, cols.shape[1])).T > 0.5
    lane = lax.broadcasted_iota(jnp.int32, is_odd.shape, 1)
    return is_odd, (lane < 64) != is_odd


def dot(a, b):
    return jnp.dot(a, b, preferred_element_type=jnp.float32)


UN_Q = 4
UN_I = 8


def local_kernel(sched, fine_agg, coarse_place, a_ref, p_ref, a_row, a_col, p_row, p_col, q_ref, cols_ref, out_ref,
                 a_dense, p_rows, p_dense, product, total, staged, mask, q_rows, out_sem):
    own_row = lax.axis_index("row")
    row_index = lax.broadcasted_iota(jnp.int32, (256, 256), 0)
    col_index = lax.broadcasted_iota(jnp.int32, (256, 256), 1)
    swap = jnp.where(col_index == (row_index % 16) * 16 + row_index // 16, 1.0, 0.0).astype(jnp.bfloat16)
    panels = (LAST, sched[0] + sched[1] - LAST)

    a_hot, a_par, p_hot, p_par = [], [], [], []
    for k in panels:
        pick = pl.ds(k, 1)
        a_hot.append(one_hot((a_col[pick, :] // 2) * FR + a_row[pick, :], 256))
        p_hot.append(one_hot((p_col[pick, :] // 2) * KB + p_row[pick, :], 128))
        a_par.append(parity(a_col[pick, :]))
        p_par.append(parity(p_col[pick, :]))

    block_of = (lax.broadcasted_iota(jnp.int32, (FR, CB * B), 1) // B).astype(jnp.float32)
    groups = cols_ref.shape[1]
    own = lax.broadcasted_iota(jnp.int32, (FR, groups), 1) == lax.broadcasted_iota(jnp.int32, (FR, groups), 0) + own_row * FR
    chosen = jnp.where(own, 1.0, 0.0).astype(jnp.bfloat16)
    picked = lax.dot_general(
        chosen, cols_ref[...].astype(jnp.float32).astype(jnp.bfloat16), (((1,), (1,)), ((), ())), preferred_element_type=jnp.float32
    )
    hit = block_of == picked[:, 0:1]
    for n in range(1, picked.shape[1]):
        hit = hit | (block_of == picked[:, n:n + 1])
    mask[...] = jnp.where(hit, 1.0, 0.0)
    for r in range(FR):
        q_rows[r * FR:(r + 1) * FR, :] = q_ref[:, r * LANES:(r + 1) * LANES].astype(jnp.float32)

    @pl.loop(0, 16, unroll=UN_Q)
    def _(q):
        lanes = pl.ds(pl.multiple_of(q * 256, 256), 256)
        for s in range(SECTIONS):
            parts = halves(p_ref[s, :, lanes], *p_par[s])
            for h in range(2):
                placed = dot(p_hot[s], parts[h]).astype(jnp.bfloat16)
                for part in range(2):
                    start = pl.multiple_of((q * 4 + part * 2 + h) * KB, KB)
                    for j in range(CB // 2):
                        p_rows[s, pl.ds(start, KB), j * LANES:(j + 1) * LANES] = placed[j * KB:(j + 1) * KB, part * LANES:(part + 1) * LANES]
            parts = halves(a_ref[s, :, lanes], *a_par[s])
            for h in range(2):
                placed = dot(a_hot[s], parts[h]).astype(jnp.bfloat16)
                for part in range(2):
                    start = pl.multiple_of((h * (B // 2) + q * 2 + part) * FR, FR)
                    for k in range(KB // 2):
                        lane = s * KB * B + k * LANES
                        a_dense[pl.ds(start, FR), lane:lane + LANES] = placed[k * FR:(k + 1) * FR, part * LANES:(part + 1) * LANES]

    for s in range(SECTIONS):
        for group in range(4):
            ordered = dot(swap, p_rows[s, group * 256:(group + 1) * 256, :]).astype(jnp.bfloat16)
            for k in range(KB):
                start = s * KB * B + k * B + group * 16
                p_dense[start:start + 16, :] = ordered[k * 16:(k + 1) * 16, :]

    for h in range(2):
        for n in range(2):

            @pl.loop(0, 4)
            def _(m):
                start = pl.multiple_of(m * 512, 512)
                lane = h * HALF + n * 256
                tile = dot(a_dense[pl.ds(start, 512), :], p_dense[:, lane:lane + 256])
                product[2 * n, pl.ds(start, 512), :] = tile[:, :LANES]
                product[2 * n + 1, pl.ds(start, 512), :] = tile[:, LANES:]

        @pl.loop(0, 64)
        def _(g):
            total[g] = jnp.zeros((B, HALF), jnp.float32)

        @pl.loop(0, FR, step=UN_I)
        def _(first):
            terms = []
            turned = []
            for t in range(4):
                groups = []
                for high in range(B // 8):
                    rows = [product[t, pl.ds(pl.multiple_of((high * 8 + low) * FR + first, 8), 8), :] for low in range(8)]
                    groups.append(jnp.swapaxes(jnp.stack(rows, axis=0), 0, 1))
                turned.append(groups)
            for u in range(UN_I):
                i = first + u
                pair = q_rows[pl.ds(i, B // 2, stride=FR), :]
                flipped = jnp.concatenate([pair, pltpu.roll(pair, 64, 1)], axis=0)[:, :B]
                lhs = jnp.concatenate([flipped, flipped], axis=0).astype(jnp.bfloat16)
                for j in range(0, 4, 2):
                    tops, bottoms = [], []
                    for t in (j, j + 1):
                        block = jnp.concatenate([group[u] for group in turned[t]], axis=0)
                        top = block.astype(jnp.bfloat16)
                        tops.append(top)
                        bottoms.append((block - top.astype(jnp.float32)).astype(jnp.bfloat16))
                    rhs = jnp.concatenate([jnp.concatenate(tops, axis=1), jnp.concatenate(bottoms, axis=1)], axis=0)
                    term = lax.dot_general(lhs, rhs, (((0,), (0,)), ((), ())), preferred_element_type=jnp.float32)
                    terms.append(term.astype(jnp.bfloat16).astype(jnp.float32))
            for u in range(UN_I):
                i = first + u
                place = coarse_place[fine_agg[own_row * FR + i]]
                owner, member = place // AGG_DEV, place % AGG_DEV
                target = place if h == 0 else ((owner % 4) * 4 + owner // 4) * AGG_DEV + member
                for j in range(0, 4, 2):
                    lanes = slice(j * LANES, (j + 2) * LANES)
                    keep = mask[pl.ds(i, 1), h * HALF + j * LANES:h * HALF + (j + 2) * LANES]
                    total[target, :, lanes] += terms[u * 2 + j // 2] * keep

        @pl.loop(0, 64)
        def _(g):
            staged[h, g] = total[g].astype(jnp.bfloat16)

        pltpu.make_async_copy(staged.at[h], out_ref.at[h], out_sem.at[h]).start()

    for h in range(2):
        pltpu.make_async_copy(staged.at[h], out_ref.at[h], out_sem.at[h]).wait()


def local_terms(sched, fine_agg, coarse_place, a, p, a_row, a_col, p_row, p_col, q, prod_cols):
    smem = pl.BlockSpec(memory_space=pltpu.SMEM)
    vmem = pl.BlockSpec(memory_space=pltpu.VMEM)
    return pl.pallas_call(
        local_kernel,
        out_shape=jax.ShapeDtypeStruct((2, 64, B, HALF), jnp.bfloat16),
        in_specs=[smem] * 3 + [vmem] * 8,
        out_specs=pl.BlockSpec(memory_space=pl.ANY),
        scratch_shapes=[
            pltpu.VMEM((FR * B, SECTIONS * KB * B), jnp.bfloat16),
            pltpu.VMEM((SECTIONS, KB * B, CB * B), jnp.bfloat16),
            pltpu.VMEM((SECTIONS * KB * B, CB * B), jnp.bfloat16),
            pltpu.VMEM((4, FR * B, LANES), jnp.float32),
            pltpu.VMEM((64, B, HALF), jnp.float32),
            pltpu.VMEM((2, 64, B, HALF), jnp.bfloat16),
            pltpu.VMEM((FR, CB * B), jnp.float32),
            pltpu.VMEM((FR * B // 2, LANES), jnp.float32),
            pltpu.SemaphoreType.DMA((2,)),
        ],
        compiler_params=pltpu.CompilerParams(vmem_limit_bytes=60 * 1024 * 1024),
        name="local_terms",
    )(sched, fine_agg, coarse_place, a, p, a_row, a_col, p_row, p_col, q, prod_cols)


def per_device(a_blocks, a_row, a_col, p_blocks, p_row, p_col, q_blocks, sched, fine_agg, coarse_place, prod_cols):
    other = jnp.sum(sched) - LAST
    a, p = lax.switch(other, [functools.partial(gather_panels, k) for k in range(LAST)], a_blocks, p_blocks)
    term = local_terms(
        sched,
        fine_agg,
        coarse_place,
        a.reshape(SECTIONS, FR * 8, B * B),
        p.reshape(SECTIONS, KB * 8, B * B),
        a_row,
        a_col,
        p_row,
        p_col,
        q_blocks,
        prod_cols.T,
    )
    return reduce_terms(term.reshape(2, 4, 4, 4, B, HALF))


def solution(mesh):
    in_specs = (
        P("col", "row", None),
        P(None, "row"),
        P(None, "row"),
        P("row", "col", None),
        P(None, "col"),
        P(None, "col"),
        P("row", None),
        P(),
        P(),
        P(),
        P(None, "col"),
    )
    return jax.shard_map(per_device, mesh=mesh, in_specs=in_specs, out_specs=P("row", "col"), check_vma=False)
```

```python
import functools

import jax
import jax.numpy as jnp
from jax import lax
from jax.experimental import pallas as pl
from jax.experimental.pallas import tpu as pltpu
from jax.sharding import PartitionSpec as P

B = 64
FR = 32
KB = 16
CB = 16
SECTIONS = 2
LANES = 128
AGG_DEV = 4


MESH = pl.DeviceIdType.MESH
LAST = 15
A_GROUPS = 16
P_GROUPS = 8
A_CUT = 1
A_LAG = 2
P_TIMES = (5, 7, 8, 10, 13)


def remote(src, dst, send_sem, recv_sem, target):
    return pltpu.make_async_remote_copy(
        src_ref=src, dst_ref=dst, send_sem=send_sem, recv_sem=recv_sem, device_id=target, device_id_type=MESH
    )


def greet(targets, distant=()):
    barrier = pltpu.get_barrier_semaphore()
    everyone = list(distant) + list(targets)
    for target in everyone:
        pl.semaphore_signal(barrier, inc=1, device_id=target, device_id_type=MESH)
    pl.semaphore_wait(barrier, len(everyone))


def place_of():
    row, col = lax.axis_index("row"), lax.axis_index("col")
    return row // 4, row % 4, col // 2, col % 2


def device(y, z, x, core):
    return (y * 4 + z, x * 2 + core)


def gather_kernel(panel, a_ref, p_ref, a_out, p_out, a_buf, p_buf, a_recv, a_fwd, a_sib, line_send, line_recv, across_send, across_recv,
                  far_send, far_recv, along_send, along_recv, relay_send, relay_recv, load_sem, out_sem):
    y, z, x, core = place_of()
    sibling = device(y, z, x, 1 - core)
    x_next = [device(y, z, (x + 1) % 4, core), device(y, z, (x + 3) % 4, core)]
    y_next = [device((y + 1) % 4, z, x, core), device((y + 3) % 4, z, x, core)]
    z_next = [device(y, (z + 1) % 4, x, core), device(y, (z + 3) % 4, x, core)]
    panels = (LAST, panel)
    chunks = A_GROUPS // 2 * A_CUT
    width = B * B // A_CUT
    parts = [pl.ds(0, B * B // 2), pl.ds(B * B // 2, B * B // 2)]

    for s, k in enumerate(panels):
        @pl.when((x == (k // 2) // 2) & (core == (k // 2) % 2))
        def _():
            pltpu.make_async_copy(a_ref.at[k % 2], a_buf.at[s], load_sem.at[0, s]).start()

        @pl.when((y == k // 4) & (z == k % 4))
        def _():
            pltpu.make_async_copy(p_ref.at[0], p_buf.at[s], load_sem.at[1, s]).start()

    greet([sibling] + x_next + y_next + z_next, [device((y + 2) % 4, z, x, core), device(y, (z + 2) % 4, x, core)])

    for s, k in enumerate(panels):
        @pl.when((y == k // 4) & (z == k % 4))
        def _():
            pltpu.make_async_copy(p_ref.at[0], p_buf.at[s], load_sem.at[1, s]).wait()

        @pl.when((x == (k // 2) // 2) & (core == (k // 2) % 2))
        def _():
            pltpu.make_async_copy(a_ref.at[k % 2], a_buf.at[s], load_sem.at[0, s]).wait()

    def a_role(k, way):
        x_root, core_root = (k // 2) // 2, (k // 2) % 2
        ahead = (x - x_root + 4) % 4 if way == 0 else (x_root - x + 4) % 4
        active = core == way
        origin = (ahead == 0) & (core == core_root)
        onward = active & (ahead < 3)
        if core_root == way:
            return ahead, origin, onward, active, A_LAG * ahead + jnp.where(active, 0, 1)
        lag = jnp.where(origin, 0, A_LAG * ahead + jnp.where(active, 1, 2))
        return ahead, origin, onward, (active & (ahead > 0)) | origin, lag

    def a_stream(s, k, way, t):
        ahead, origin, onward, sideways, lag = a_role(k, way)
        g = t - lag

        @pl.when((g >= 0) & (g < chunks))
        def _():
            block = way * (A_GROUPS // 2) + g // A_CUT
            lanes = pl.ds(pl.multiple_of((g % A_CUT) * width, width), width)
            here = a_buf.at[s, block, :, lanes]
            arrival = a_recv.at[s, way * chunks + g]

            @pl.when(jnp.logical_not(origin))
            def _():
                remote(here, here, a_fwd.at[s, way], arrival, sibling).wait_recv()

            @pl.when(onward)
            def _():
                remote(here, here, a_fwd.at[s, way], arrival, x_next[way]).start()

            @pl.when(sideways)
            def _():
                remote(here, here, a_sib.at[s, way], arrival, sibling).start()

            pltpu.make_async_copy(here, a_out.at[s, block, :, lanes], out_sem.at[0]).start()

    def p_role(k, f):
        if f == 0:
            u, w, u_root, w_root, u_next, w_next = y, z, k // 4, k % 4, y_next, z_next
        else:
            u, w, u_root, w_root, u_next, w_next = z, y, k % 4, k // 4, z_next, y_next
        du, dw = (u - u_root + 4) % 4, (w - w_root + 4) % 4
        clear = [jnp.logical_not((dw == 0) & (du == 3)), jnp.logical_not((dw == 0) & (du == 1))]
        return u, u_root, w_root, u_next, w_next, du, dw, clear

    pairs = [(s, k, f) for s, k in enumerate(panels) for f in range(2)]

    def along(s, f, u, u_next, clear):
        group = p_buf.at[s, f * 4 + u]
        for d in range(2):
            @pl.when(clear[d])
            def _():
                remote(group, group, along_send.at[s, f, d], along_recv.at[s, f, d], u_next[d]).start()

    def relay(s, f, u, u_next, clear, d):
        group = p_buf.at[s, f * 4 + (u + (3 if d == 0 else 1)) % 4, :, parts[d]]

        @pl.when(clear[d])
        def _():
            remote(group, group, relay_send.at[s, f, d], relay_recv.at[s, f, d], u_next[d]).start()

    def across(s, f, u, w_next):
        group = p_buf.at[s, f * 4 + u]
        for d in range(2):
            remote(group, group, across_send.at[s, f, d], across_recv.at[s, f, d], w_next[d]).start()

    for s, k, f in pairs:
        u, u_root, w_root, u_next, w_next, du, dw, clear = p_role(k, f)

        @pl.when((du == 0) & (dw == 0))
        def _():
            for j in (2, 1, 3):
                g = (u_root + j) % 4
                group = p_buf.at[s, f * 4 + g]
                target = device(g, w_root, x, core) if f == 0 else device(w_root, g, x, core)
                remote(group, group, line_send.at[s, f, j - 1], line_recv.at[s, f], target).start()
            across(s, f, u, w_next)
            along(s, f, u, u_next, clear)
            for d in range(2):
                relay(s, f, u, u_next, clear, d)

    def first_arrivals():
        for s, k, f in pairs:
            u, u_root, w_root, u_next, w_next, du, dw, clear = p_role(k, f)

            @pl.when((du != 0) & (dw == 0))
            def _():
                group = p_buf.at[s, f * 4 + u]
                remote(group, group, line_send.at[s, f, 0], line_recv.at[s, f], sibling).wait_recv()
                across(s, f, u, w_next)
                along(s, f, u, u_next, clear)

    def second_arrivals():
        for s, k, f in pairs:
            u, u_root, w_root, u_next, w_next, du, dw, clear = p_role(k, f)
            for d in range(2):
                @pl.when(dw == (1 if d == 0 else 3))
                def _():
                    group = p_buf.at[s, f * 4 + u]
                    remote(group, group, across_send.at[s, f, d], across_recv.at[s, f, d], sibling).wait_recv()
                    half = p_buf.at[s, f * 4 + u, :, parts[d]]
                    remote(half, half, far_send.at[s, f, d], far_recv.at[s, f, d], w_next[d]).start()
                    along(s, f, u, u_next, clear)

    def third_arrivals():
        for s, k, f in pairs:
            u, u_root, w_root, u_next, w_next, du, dw, clear = p_role(k, f)

            @pl.when(dw == 2)
            def _():
                for d in range(2):
                    half = p_buf.at[s, f * 4 + u, :, parts[d]]
                    remote(half, half, far_send.at[s, f, d], far_recv.at[s, f, d], sibling).wait_recv()
                along(s, f, u, u_next, clear)

    def fourth_arrivals():
        for s, k, f in pairs:
            u, u_root, w_root, u_next, w_next, du, dw, clear = p_role(k, f)

            @pl.when((du != 0) | (dw != 0))
            def _():
                for d in range(2):
                    group = p_buf.at[s, f * 4 + (u + (3 if d == 0 else 1)) % 4]
                    remote(group, group, along_send.at[s, f, d], along_recv.at[s, f, d], sibling).wait_recv()
                    relay(s, f, u, u_next, clear, d)

    def last_arrivals():
        for s, k, f in pairs:
            u, u_root, w_root, u_next, w_next, du, dw, clear = p_role(k, f)

            @pl.when((du != 0) | (dw != 0))
            def _():
                for d in range(2):
                    group = p_buf.at[s, f * 4 + (u + 2) % 4, :, parts[d]]
                    remote(group, group, relay_send.at[s, f, d], relay_recv.at[s, f, d], sibling).wait_recv()

        pltpu.make_async_copy(p_buf, p_out, out_sem.at[1]).start()

    @pl.loop(0, chunks + 3 * A_LAG + 2)
    def _(t):
        for s, k in enumerate(panels):
            for way in range(2):
                a_stream(s, k, way, t)
        for when, act in zip(P_TIMES, (first_arrivals, second_arrivals, third_arrivals, fourth_arrivals, last_arrivals)):
            pl.when(t == when)(act)

    for s, k in enumerate(panels):
        for way in range(2):
            ahead, origin, onward, sideways, lag = a_role(k, way)
            half = a_buf.at[s, pl.ds(way * (A_GROUPS // 2), A_GROUPS // 2)]

            @pl.when(onward)
            def _():
                remote(half, half, a_fwd.at[s, way], a_recv.at[s, 0], sibling).wait_send()

            @pl.when(sideways)
            def _():
                remote(half, half, a_sib.at[s, way], a_recv.at[s, 0], sibling).wait_send()

    for s, k, f in pairs:
        u, u_root, w_root, u_next, w_next, du, dw, clear = p_role(k, f)
        group = p_buf.at[s, f * 4 + u]
        half = p_buf.at[s, f * 4 + u, :, parts[0]]

        @pl.when((du == 0) & (dw == 0))
        def _():
            for j in range(3):
                remote(group, group, line_send.at[s, f, j], line_recv.at[s, f], sibling).wait_send()

        for d in range(2):
            @pl.when(dw == 0)
            def _():
                remote(group, group, across_send.at[s, f, d], across_recv.at[s, f, d], sibling).wait_send()

            @pl.when(dw == (1 if d == 0 else 3))
            def _():
                remote(half, half, far_send.at[s, f, d], far_recv.at[s, f, d], sibling).wait_send()

            @pl.when(clear[d])
            def _():
                remote(group, group, along_send.at[s, f, d], along_recv.at[s, f, d], sibling).wait_send()
                remote(half, half, relay_send.at[s, f, d], relay_recv.at[s, f, d], sibling).wait_send()

    pltpu.make_async_copy(a_buf, a_out, out_sem.at[0]).wait()
    pltpu.make_async_copy(p_buf, p_out, out_sem.at[1]).wait()


def gather_panels(panel, a_blocks, p_blocks):
    anywhere = pl.BlockSpec(memory_space=pl.ANY)
    a_shape = (SECTIONS, A_GROUPS, 16, B * B)
    p_shape = (SECTIONS, P_GROUPS, 16, B * B)
    dma = pltpu.SemaphoreType.DMA
    ends = [dma((SECTIONS, 2, 2)), dma((SECTIONS, 2, 2))]
    return pl.pallas_call(
        functools.partial(gather_kernel, panel),
        out_shape=(jax.ShapeDtypeStruct(a_shape, jnp.bfloat16), jax.ShapeDtypeStruct(p_shape, jnp.bfloat16)),
        in_specs=[anywhere] * 2,
        out_specs=(anywhere, anywhere),
        scratch_shapes=[
            pltpu.VMEM(a_shape, jnp.bfloat16),
            pltpu.VMEM(p_shape, jnp.bfloat16),
            dma((SECTIONS, A_GROUPS * A_CUT)),
            dma((SECTIONS, 2)),
            dma((SECTIONS, 2)),
            dma((SECTIONS, 2, 3)),
            dma((SECTIONS, 2)),
        ]
        + ends * 4
        + [dma((2, SECTIONS)), dma((2,))],
        compiler_params=pltpu.CompilerParams(collective_id=1 + panel, has_side_effects=True, vmem_limit_bytes=16 * 1024 * 1024),
        name=f"gather_{panel}",
    )(a_blocks.reshape(2, A_GROUPS, 16, B * B), p_blocks.reshape(1, P_GROUPS, 16, B * B))


HALF = 512
PART = AGG_DEV * B


def add_rows(total, extra, count):
    @pl.loop(0, count)
    def _(i):
        total[i] = (total[i].astype(jnp.float32) + extra[i].astype(jnp.float32)).astype(jnp.bfloat16)


def reduce_kernel(t_ref, o_ref, own, fwd, in_a, in_b, mid, in2_a, in2_b, local_sem, send, recv, send2, recv2):
    y, z, x, core = place_of()
    y_next = [device((y + 1) % 4, z, x, core), device((y + 3) % 4, z, x, core)]
    z_next = [device(y, (z + 1) % 4, x, core), device(y, (z + 3) % 4, x, core)]
    greet(y_next + z_next)
    here = ((y, z), (z, y))
    nexts = ((y_next, z_next), (z_next, y_next))

    started = []
    for h in range(2):
        u = here[h][0]
        for d in range(2):
            step = (u + 1) % 4 if d == 0 else (u + 3) % 4
            copy = remote(t_ref.at[h, (u + 2) % 4, pl.ds(2 * d, 2)], in_a.at[h, d], send.at[h, d, 0], recv.at[h, d, 0], nexts[h][0][d])
            copy.start()
            started.append(copy)
    for h in range(2):
        u = here[h][0]
        for d in range(2):
            step = (u + 1) % 4 if d == 0 else (u + 3) % 4
            other = 2 * (1 - d)
            copy = remote(t_ref.at[h, step, pl.ds(other, 2)], in_b.at[h, d, pl.ds(other, 2)], send.at[h, d, 1], recv.at[h, d, 1], nexts[h][0][d])
            copy.start()
            started.append(copy)
            pltpu.make_async_copy(t_ref.at[h, step, pl.ds(2 * d, 2)], fwd.at[h, d], local_sem.at[h, d]).start()
        pltpu.make_async_copy(t_ref.at[h, u], own.at[h], local_sem.at[h, 2]).start()

    for h in range(2):
        u = here[h][0]
        for d in range(2):
            step = (u + 1) % 4 if d == 0 else (u + 3) % 4
            pltpu.make_async_copy(t_ref.at[h, step, pl.ds(2 * d, 2)], fwd.at[h, d], local_sem.at[h, d]).wait()
            remote(in_a.at[h, d], in_a.at[h, d], send.at[h, d, 0], recv.at[h, d, 0], nexts[h][0][d]).wait_recv()
            for part in range(2):
                add_rows(fwd.at[h, d, part], in_a.at[h, d, part], 4)
            copy = remote(fwd.at[h, d], in_b.at[h, d, pl.ds(2 * d, 2)], send.at[h, d, 2], recv.at[h, d, 2], nexts[h][0][d])
            copy.start()
            started.append(copy)

    def summed(h, part, i):
        first = own[h, part, i].astype(jnp.float32) + in_b[h, 0, part, i].astype(jnp.float32)
        return first + in_b[h, 1, part, i].astype(jnp.float32)

    for h in range(2):
        u, w = here[h]
        pltpu.make_async_copy(t_ref.at[h, u], own.at[h], local_sem.at[h, 2]).wait()
        for d in range(2):
            other = 2 * (1 - d)
            for part, index in ((other, 1), (2 * d, 2)):
                block = in_b.at[h, d, pl.ds(part, 2)]
                remote(block, block, send.at[h, d, index], recv.at[h, d, index], nexts[h][0][d]).wait_recv()

        opposite = (w + 2) % 4

        @pl.loop(0, 4)
        def _(i):
            mid[h, 2, i] = summed(h, opposite, i).astype(jnp.bfloat16)

        for d in range(2):
            copy = remote(mid.at[h, 2, pl.ds(2 * d, 2)], in2_a.at[h, d], send2.at[h, d, 0], recv2.at[h, d, 0], nexts[h][1][d])
            copy.start()
            started.append(copy)
        for d in range(2):
            step = (w + 1) % 4 if d == 0 else (w + 3) % 4
            other = 2 * (1 - d)

            @pl.loop(0, 2)
            def _(i):
                mid[h, d, other + i] = summed(h, step, other + i).astype(jnp.bfloat16)

            block = pl.ds(other, 2)
            copy = remote(mid.at[h, d, block], in2_b.at[h, d, block], send2.at[h, d, 1], recv2.at[h, d, 1], nexts[h][1][d])
            copy.start()
            started.append(copy)

    for h in range(2):
        u, w = here[h]
        for d in range(2):
            step = (w + 1) % 4 if d == 0 else (w + 3) % 4
            remote(in2_a.at[h, d], in2_a.at[h, d], send2.at[h, d, 0], recv2.at[h, d, 0], nexts[h][1][d]).wait_recv()

            @pl.loop(0, 2)
            def _(i):
                mid[h, d, 2 * d + i] = (summed(h, step, 2 * d + i) + in2_a[h, d, i].astype(jnp.float32)).astype(jnp.bfloat16)

            block = pl.ds(2 * d, 2)
            copy = remote(mid.at[h, d, block], in2_b.at[h, d, block], send2.at[h, d, 2], recv2.at[h, d, 2], nexts[h][1][d])
            copy.start()
            started.append(copy)

    for h in range(2):
        u, w = here[h]
        for d in range(2):
            other = 2 * (1 - d)
            for part, index in ((other, 1), (2 * d, 2)):
                block = in2_b.at[h, d, pl.ds(part, 2)]
                remote(block, block, send2.at[h, d, index], recv2.at[h, d, index], nexts[h][1][d]).wait_recv()

        @pl.loop(0, 4)
        def _(i):
            value = summed(h, w, i) + in2_b[h, 0, i].astype(jnp.float32) + in2_b[h, 1, i].astype(jnp.float32)
            o_ref[pl.ds(pl.multiple_of(i * B, B), B), h * HALF:(h + 1) * HALF] = value

    for copy in started:
        copy.wait_send()


def reduce_terms(term):
    return pl.pallas_call(
        reduce_kernel,
        out_shape=jax.ShapeDtypeStruct((PART, 2 * HALF), jnp.float32),
        in_specs=[pl.BlockSpec(memory_space=pl.ANY)],
        out_specs=pl.BlockSpec(memory_space=pltpu.VMEM),
        scratch_shapes=[
            pltpu.VMEM((2, 4, 4, B, HALF), jnp.bfloat16),
            pltpu.VMEM((2, 2, 2, 4, B, HALF), jnp.bfloat16),
            pltpu.VMEM((2, 2, 2, 4, B, HALF), jnp.bfloat16),
            pltpu.VMEM((2, 2, 4, 4, B, HALF), jnp.bfloat16),
            pltpu.VMEM((2, 3, 4, B, HALF), jnp.bfloat16),
            pltpu.VMEM((2, 2, 2, B, HALF), jnp.bfloat16),
            pltpu.VMEM((2, 2, 4, B, HALF), jnp.bfloat16),
            pltpu.SemaphoreType.DMA((2, 3)),
            pltpu.SemaphoreType.DMA((2, 2, 3)),
            pltpu.SemaphoreType.DMA((2, 2, 3)),
            pltpu.SemaphoreType.DMA((2, 2, 3)),
            pltpu.SemaphoreType.DMA((2, 2, 3)),
        ],
        compiler_params=pltpu.CompilerParams(collective_id=0, has_side_effects=True, vmem_limit_bytes=16 * 1024 * 1024),
        name="reduce_terms",
    )(term)


def halves(x, is_odd, keep):
    evens, odds = [], []
    for part in range(2):
        own = x[:, part * LANES:(part + 1) * LANES].astype(jnp.float32)
        swapped = pltpu.roll(own, 64, 1)
        evens.append(jnp.where(keep, jnp.where(is_odd, swapped, own), 0.0).astype(jnp.bfloat16))
        odds.append(jnp.where(keep, jnp.where(is_odd, own, swapped), 0.0).astype(jnp.bfloat16))
    return jnp.concatenate(evens, axis=1), jnp.concatenate(odds, axis=1)


def one_hot(position, count):
    rows = lax.broadcasted_iota(jnp.int32, (count, position.shape[1]), 0)
    return jnp.where(rows == position, 1.0, 0.0).astype(jnp.bfloat16)


def parity(cols):
    odd = (cols % 2).astype(jnp.float32)
    is_odd = jnp.broadcast_to(odd, (LANES, cols.shape[1])).T > 0.5
    lane = lax.broadcasted_iota(jnp.int32, is_odd.shape, 1)
    return is_odd, (lane < 64) != is_odd


def dot(a, b):
    return jnp.dot(a, b, preferred_element_type=jnp.float32)


UN_Q = 4
UN_I = 8


def local_kernel(sched, fine_agg, coarse_place, a_ref, p_ref, a_row, a_col, p_row, p_col, q_ref, cols_ref, out_ref,
                 a_dense, p_rows, p_dense, product, total, mask, q_rows):
    own_row = lax.axis_index("row")
    row_index = lax.broadcasted_iota(jnp.int32, (256, 256), 0)
    col_index = lax.broadcasted_iota(jnp.int32, (256, 256), 1)
    swap = jnp.where(col_index == (row_index % 16) * 16 + row_index // 16, 1.0, 0.0).astype(jnp.bfloat16)
    panels = (LAST, sched[0] + sched[1] - LAST)

    a_hot, a_par, p_hot, p_par = [], [], [], []
    for k in panels:
        pick = pl.ds(k, 1)
        a_hot.append(one_hot((a_col[pick, :] // 2) * FR + a_row[pick, :], 256))
        p_hot.append(one_hot((p_col[pick, :] // 2) * KB + p_row[pick, :], 128))
        a_par.append(parity(a_col[pick, :]))
        p_par.append(parity(p_col[pick, :]))

    block_of = (lax.broadcasted_iota(jnp.int32, (FR, CB * B), 1) // B).astype(jnp.float32)
    groups = cols_ref.shape[1]
    own = lax.broadcasted_iota(jnp.int32, (FR, groups), 1) == lax.broadcasted_iota(jnp.int32, (FR, groups), 0) + own_row * FR
    chosen = jnp.where(own, 1.0, 0.0).astype(jnp.bfloat16)
    picked = lax.dot_general(
        chosen, cols_ref[...].astype(jnp.float32).astype(jnp.bfloat16), (((1,), (1,)), ((), ())), preferred_element_type=jnp.float32
    )
    hit = block_of == picked[:, 0:1]
    for n in range(1, picked.shape[1]):
        hit = hit | (block_of == picked[:, n:n + 1])
    mask[...] = jnp.where(hit, 1.0, 0.0)
    for r in range(FR):
        q_rows[r * FR:(r + 1) * FR, :] = q_ref[:, r * LANES:(r + 1) * LANES].astype(jnp.float32)

    @pl.loop(0, 16, unroll=UN_Q)
    def _(q):
        lanes = pl.ds(pl.multiple_of(q * 256, 256), 256)
        for s in range(SECTIONS):
            parts = halves(p_ref[s, :, lanes], *p_par[s])
            for h in range(2):
                placed = dot(p_hot[s], parts[h]).astype(jnp.bfloat16)
                for part in range(2):
                    start = pl.multiple_of((q * 4 + part * 2 + h) * KB, KB)
                    for j in range(CB // 2):
                        p_rows[s, pl.ds(start, KB), j * LANES:(j + 1) * LANES] = placed[j * KB:(j + 1) * KB, part * LANES:(part + 1) * LANES]
            parts = halves(a_ref[s, :, lanes], *a_par[s])
            for h in range(2):
                placed = dot(a_hot[s], parts[h]).astype(jnp.bfloat16)
                for part in range(2):
                    start = pl.multiple_of((h * (B // 2) + q * 2 + part) * FR, FR)
                    for k in range(KB // 2):
                        lane = s * KB * B + k * LANES
                        a_dense[pl.ds(start, FR), lane:lane + LANES] = placed[k * FR:(k + 1) * FR, part * LANES:(part + 1) * LANES]

    for s in range(SECTIONS):
        for group in range(4):
            ordered = dot(swap, p_rows[s, group * 256:(group + 1) * 256, :]).astype(jnp.bfloat16)
            for k in range(KB):
                start = s * KB * B + k * B + group * 16
                p_dense[start:start + 16, :] = ordered[k * 16:(k + 1) * 16, :]

    for h in range(2):
        for n in range(2):

            @pl.loop(0, 4)
            def _(m):
                start = pl.multiple_of(m * 512, 512)
                lane = h * HALF + n * 256
                tile = dot(a_dense[pl.ds(start, 512), :], p_dense[:, lane:lane + 256])
                product[2 * n, pl.ds(start, 512), :] = tile[:, :LANES]
                product[2 * n + 1, pl.ds(start, 512), :] = tile[:, LANES:]

        @pl.loop(0, 64)
        def _(g):
            total[g] = jnp.zeros((B, HALF), jnp.float32)

        @pl.loop(0, FR, step=UN_I)
        def _(first):
            terms = []
            turned = []
            for t in range(4):
                groups = []
                for high in range(B // 8):
                    rows = [product[t, pl.ds(pl.multiple_of((high * 8 + low) * FR + first, 8), 8), :] for low in range(8)]
                    groups.append(jnp.swapaxes(jnp.stack(rows, axis=0), 0, 1))
                turned.append(groups)
            for u in range(UN_I):
                i = first + u
                pair = q_rows[pl.ds(i, B // 2, stride=FR), :]
                flipped = jnp.concatenate([pair, pltpu.roll(pair, 64, 1)], axis=0)[:, :B]
                lhs = jnp.concatenate([flipped, flipped], axis=0).astype(jnp.bfloat16)
                for j in range(0, 4, 2):
                    tops, bottoms = [], []
                    for t in (j, j + 1):
                        block = jnp.concatenate([group[u] for group in turned[t]], axis=0)
                        top = block.astype(jnp.bfloat16)
                        tops.append(top)
                        bottoms.append((block - top.astype(jnp.float32)).astype(jnp.bfloat16))
                    rhs = jnp.concatenate([jnp.concatenate(tops, axis=1), jnp.concatenate(bottoms, axis=1)], axis=0)
                    term = lax.dot_general(lhs, rhs, (((0,), (0,)), ((), ())), preferred_element_type=jnp.float32)
                    terms.append(term.astype(jnp.bfloat16).astype(jnp.float32))
            for u in range(UN_I):
                i = first + u
                place = coarse_place[fine_agg[own_row * FR + i]]
                owner, member = place // AGG_DEV, place % AGG_DEV
                target = place if h == 0 else ((owner % 4) * 4 + owner // 4) * AGG_DEV + member
                for j in range(0, 4, 2):
                    lanes = slice(j * LANES, (j + 2) * LANES)
                    keep = mask[pl.ds(i, 1), h * HALF + j * LANES:h * HALF + (j + 2) * LANES]
                    total[target, :, lanes] += terms[u * 2 + j // 2] * keep

        @pl.loop(0, 64)
        def _(g):
            out_ref[h, g] = total[g].astype(jnp.bfloat16)


def local_terms(sched, fine_agg, coarse_place, a, p, a_row, a_col, p_row, p_col, q, prod_cols):
    smem = pl.BlockSpec(memory_space=pltpu.SMEM)
    vmem = pl.BlockSpec(memory_space=pltpu.VMEM)
    return pl.pallas_call(
        local_kernel,
        out_shape=jax.ShapeDtypeStruct((2, 64, B, HALF), jnp.bfloat16),
        in_specs=[smem] * 3 + [vmem] * 8,
        out_specs=vmem,
        scratch_shapes=[
            pltpu.VMEM((FR * B, SECTIONS * KB * B), jnp.bfloat16),
            pltpu.VMEM((SECTIONS, KB * B, CB * B), jnp.bfloat16),
            pltpu.VMEM((SECTIONS * KB * B, CB * B), jnp.bfloat16),
            pltpu.VMEM((4, FR * B, LANES), jnp.float32),
            pltpu.VMEM((64, B, HALF), jnp.float32),
            pltpu.VMEM((FR, CB * B), jnp.float32),
            pltpu.VMEM((FR * B // 2, LANES), jnp.float32),
        ],
        compiler_params=pltpu.CompilerParams(vmem_limit_bytes=44 * 1024 * 1024),
        name="local_terms",
    )(sched, fine_agg, coarse_place, a, p, a_row, a_col, p_row, p_col, q, prod_cols)


def per_device(a_blocks, a_row, a_col, p_blocks, p_row, p_col, q_blocks, sched, fine_agg, coarse_place, prod_cols):
    other = jnp.sum(sched) - LAST
    a, p = lax.switch(other, [functools.partial(gather_panels, k) for k in range(LAST)], a_blocks, p_blocks)
    term = local_terms(
        sched,
        fine_agg,
        coarse_place,
        a.reshape(SECTIONS, FR * 8, B * B),
        p.reshape(SECTIONS, KB * 8, B * B),
        a_row,
        a_col,
        p_row,
        p_col,
        q_blocks,
        prod_cols.T,
    )
    return reduce_terms(term.reshape(2, 4, 4, 4, B, HALF))


def solution(mesh):
    in_specs = (
        P("col", "row", None),
        P(None, "row"),
        P(None, "row"),
        P("row", "col", None),
        P(None, "col"),
        P(None, "col"),
        P("row", None),
        P(),
        P(),
        P(),
        P(None, "col"),
    )
    return jax.shard_map(per_device, mesh=mesh, in_specs=in_specs, out_specs=P("row", "col"), check_vma=False)
```

```python
import functools

import jax
import jax.numpy as jnp
from jax import lax
from jax.experimental import pallas as pl
from jax.experimental.pallas import tpu as pltpu
from jax.sharding import PartitionSpec as P

B = 64
FR = 32
KB = 16
CB = 16
SECTIONS = 2
LANES = 128
AGG_DEV = 4


MESH = pl.DeviceIdType.MESH
LAST = 15
A_GROUPS = 16
P_GROUPS = 8
A_CUT = 1
A_LAG = 2
P_TIMES = (4, 7, 9, 12, 15)


def remote(src, dst, send_sem, recv_sem, target):
    return pltpu.make_async_remote_copy(
        src_ref=src, dst_ref=dst, send_sem=send_sem, recv_sem=recv_sem, device_id=target, device_id_type=MESH
    )


def greet(targets, distant=()):
    barrier = pltpu.get_barrier_semaphore()
    everyone = list(distant) + list(targets)
    for target in everyone:
        pl.semaphore_signal(barrier, inc=1, device_id=target, device_id_type=MESH)
    pl.semaphore_wait(barrier, len(everyone))


def place_of():
    row, col = lax.axis_index("row"), lax.axis_index("col")
    return row // 4, row % 4, col // 2, col % 2


def device(y, z, x, core):
    return (y * 4 + z, x * 2 + core)


def gather_kernel(panel, a_ref, p_ref, a_out, p_out, a_buf, p_buf, a_recv, a_fwd, a_sib, line_send, line_recv, across_send, across_recv,
                  far_send, far_recv, along_send, along_recv, relay_send, relay_recv, load_sem, out_sem):
    y, z, x, core = place_of()
    sibling = device(y, z, x, 1 - core)
    x_next = [device(y, z, (x + 1) % 4, core), device(y, z, (x + 3) % 4, core)]
    y_next = [device((y + 1) % 4, z, x, core), device((y + 3) % 4, z, x, core)]
    z_next = [device(y, (z + 1) % 4, x, core), device(y, (z + 3) % 4, x, core)]
    panels = (LAST, panel)
    chunks = A_GROUPS // 2 * A_CUT
    width = B * B // A_CUT
    parts = [pl.ds(0, B * B // 2), pl.ds(B * B // 2, B * B // 2)]

    for s, k in enumerate(panels):
        @pl.when((x == (k // 2) // 2) & (core == (k // 2) % 2))
        def _():
            pltpu.make_async_copy(a_ref.at[k % 2], a_buf.at[s], load_sem.at[0, s]).start()

        @pl.when((y == k // 4) & (z == k % 4))
        def _():
            pltpu.make_async_copy(p_ref.at[0], p_buf.at[s], load_sem.at[1, s]).start()

    greet([sibling] + x_next + y_next + z_next, [device((y + 2) % 4, z, x, core), device(y, (z + 2) % 4, x, core)])

    for s, k in enumerate(panels):
        @pl.when((y == k // 4) & (z == k % 4))
        def _():
            pltpu.make_async_copy(p_ref.at[0], p_buf.at[s], load_sem.at[1, s]).wait()

        @pl.when((x == (k // 2) // 2) & (core == (k // 2) % 2))
        def _():
            pltpu.make_async_copy(a_ref.at[k % 2], a_buf.at[s], load_sem.at[0, s]).wait()

    def a_role(k, way):
        x_root, core_root = (k // 2) // 2, (k // 2) % 2
        ahead = (x - x_root + 4) % 4 if way == 0 else (x_root - x + 4) % 4
        active = core == way
        origin = (ahead == 0) & (core == core_root)
        onward = active & (ahead < 3)
        if core_root == way:
            return ahead, origin, onward, active, A_LAG * ahead + jnp.where(active, 0, 1)
        lag = jnp.where(origin, 0, A_LAG * ahead + jnp.where(active, 1, 2))
        return ahead, origin, onward, (active & (ahead > 0)) | origin, lag

    def a_stream(s, k, way, t):
        ahead, origin, onward, sideways, lag = a_role(k, way)
        g = t - lag

        @pl.when((g >= 0) & (g < chunks))
        def _():
            block = way * (A_GROUPS // 2) + g // A_CUT
            lanes = pl.ds(pl.multiple_of((g % A_CUT) * width, width), width)
            here = a_buf.at[s, block, :, lanes]
            arrival = a_recv.at[s, way * chunks + g]

            @pl.when(jnp.logical_not(origin))
            def _():
                remote(here, here, a_fwd.at[s, way], arrival, sibling).wait_recv()

            @pl.when(onward)
            def _():
                remote(here, here, a_fwd.at[s, way], arrival, x_next[way]).start()

            @pl.when(sideways)
            def _():
                remote(here, here, a_sib.at[s, way], arrival, sibling).start()

            pltpu.make_async_copy(here, a_out.at[s, block, :, lanes], out_sem.at[0]).start()

    def p_role(k, f):
        if f == 0:
            u, w, u_root, w_root, u_next, w_next = y, z, k // 4, k % 4, y_next, z_next
        else:
            u, w, u_root, w_root, u_next, w_next = z, y, k % 4, k // 4, z_next, y_next
        du, dw = (u - u_root + 4) % 4, (w - w_root + 4) % 4
        clear = [jnp.logical_not((dw == 0) & (du == 3)), jnp.logical_not((dw == 0) & (du == 1))]
        return u, u_root, w_root, u_next, w_next, du, dw, clear

    pairs = [(s, k, f) for s, k in enumerate(panels) for f in range(2)]

    def along(s, f, u, u_next, clear):
        group = p_buf.at[s, f * 4 + u]
        for d in range(2):
            @pl.when(clear[d])
            def _():
                remote(group, group, along_send.at[s, f, d], along_recv.at[s, f, d], u_next[d]).start()

    def relay(s, f, u, u_next, clear, d):
        group = p_buf.at[s, f * 4 + (u + (3 if d == 0 else 1)) % 4, :, parts[d]]

        @pl.when(clear[d])
        def _():
            remote(group, group, relay_send.at[s, f, d], relay_recv.at[s, f, d], u_next[d]).start()

    def across(s, f, u, w_next):
        group = p_buf.at[s, f * 4 + u]
        for d in range(2):
            remote(group, group, across_send.at[s, f, d], across_recv.at[s, f, d], w_next[d]).start()

    for s, k, f in pairs:
        u, u_root, w_root, u_next, w_next, du, dw, clear = p_role(k, f)

        @pl.when((du == 0) & (dw == 0))
        def _():
            for j in (2, 1, 3):
                g = (u_root + j) % 4
                group = p_buf.at[s, f * 4 + g]
                target = device(g, w_root, x, core) if f == 0 else device(w_root, g, x, core)
                remote(group, group, line_send.at[s, f, j - 1], line_recv.at[s, f], target).start()
            across(s, f, u, w_next)
            along(s, f, u, u_next, clear)
            for d in range(2):
                relay(s, f, u, u_next, clear, d)

    def first_arrivals():
        for s, k, f in pairs:
            u, u_root, w_root, u_next, w_next, du, dw, clear = p_role(k, f)

            @pl.when((du != 0) & (dw == 0))
            def _():
                group = p_buf.at[s, f * 4 + u]
                remote(group, group, line_send.at[s, f, 0], line_recv.at[s, f], sibling).wait_recv()
                across(s, f, u, w_next)
                along(s, f, u, u_next, clear)

    def second_arrivals():
        for s, k, f in pairs:
            u, u_root, w_root, u_next, w_next, du, dw, clear = p_role(k, f)
            for d in range(2):
                @pl.when(dw == (1 if d == 0 else 3))
                def _():
                    group = p_buf.at[s, f * 4 + u]
                    remote(group, group, across_send.at[s, f, d], across_recv.at[s, f, d], sibling).wait_recv()
                    half = p_buf.at[s, f * 4 + u, :, parts[d]]
                    remote(half, half, far_send.at[s, f, d], far_recv.at[s, f, d], w_next[d]).start()
                    along(s, f, u, u_next, clear)

    def third_arrivals():
        for s, k, f in pairs:
            u, u_root, w_root, u_next, w_next, du, dw, clear = p_role(k, f)

            @pl.when(dw == 2)
            def _():
                for d in range(2):
                    half = p_buf.at[s, f * 4 + u, :, parts[d]]
                    remote(half, half, far_send.at[s, f, d], far_recv.at[s, f, d], sibling).wait_recv()
                along(s, f, u, u_next, clear)

    def fourth_arrivals():
        for s, k, f in pairs:
            u, u_root, w_root, u_next, w_next, du, dw, clear = p_role(k, f)

            @pl.when((du != 0) | (dw != 0))
            def _():
                for d in range(2):
                    group = p_buf.at[s, f * 4 + (u + (3 if d == 0 else 1)) % 4]
                    remote(group, group, along_send.at[s, f, d], along_recv.at[s, f, d], sibling).wait_recv()
                    relay(s, f, u, u_next, clear, d)

    def last_arrivals():
        for s, k, f in pairs:
            u, u_root, w_root, u_next, w_next, du, dw, clear = p_role(k, f)

            @pl.when((du != 0) | (dw != 0))
            def _():
                for d in range(2):
                    group = p_buf.at[s, f * 4 + (u + 2) % 4, :, parts[d]]
                    remote(group, group, relay_send.at[s, f, d], relay_recv.at[s, f, d], sibling).wait_recv()

        pltpu.make_async_copy(p_buf, p_out, out_sem.at[1]).start()

    @pl.loop(0, chunks + 3 * A_LAG + 2)
    def _(t):
        for s, k in enumerate(panels):
            for way in range(2):
                a_stream(s, k, way, t)
        for when, act in zip(P_TIMES, (first_arrivals, second_arrivals, third_arrivals, fourth_arrivals, last_arrivals)):
            pl.when(t == when)(act)

    for s, k in enumerate(panels):
        for way in range(2):
            ahead, origin, onward, sideways, lag = a_role(k, way)
            half = a_buf.at[s, pl.ds(way * (A_GROUPS // 2), A_GROUPS // 2)]

            @pl.when(onward)
            def _():
                remote(half, half, a_fwd.at[s, way], a_recv.at[s, 0], sibling).wait_send()

            @pl.when(sideways)
            def _():
                remote(half, half, a_sib.at[s, way], a_recv.at[s, 0], sibling).wait_send()

    for s, k, f in pairs:
        u, u_root, w_root, u_next, w_next, du, dw, clear = p_role(k, f)
        group = p_buf.at[s, f * 4 + u]
        half = p_buf.at[s, f * 4 + u, :, parts[0]]

        @pl.when((du == 0) & (dw == 0))
        def _():
            for j in range(3):
                remote(group, group, line_send.at[s, f, j], line_recv.at[s, f], sibling).wait_send()

        for d in range(2):
            @pl.when(dw == 0)
            def _():
                remote(group, group, across_send.at[s, f, d], across_recv.at[s, f, d], sibling).wait_send()

            @pl.when(dw == (1 if d == 0 else 3))
            def _():
                remote(half, half, far_send.at[s, f, d], far_recv.at[s, f, d], sibling).wait_send()

            @pl.when(clear[d])
            def _():
                remote(group, group, along_send.at[s, f, d], along_recv.at[s, f, d], sibling).wait_send()
                remote(half, half, relay_send.at[s, f, d], relay_recv.at[s, f, d], sibling).wait_send()

    pltpu.make_async_copy(a_buf, a_out, out_sem.at[0]).wait()
    pltpu.make_async_copy(p_buf, p_out, out_sem.at[1]).wait()


def gather_panels(panel, a_blocks, p_blocks):
    anywhere = pl.BlockSpec(memory_space=pl.ANY)
    a_shape = (SECTIONS, A_GROUPS, 16, B * B)
    p_shape = (SECTIONS, P_GROUPS, 16, B * B)
    dma = pltpu.SemaphoreType.DMA
    ends = [dma((SECTIONS, 2, 2)), dma((SECTIONS, 2, 2))]
    return pl.pallas_call(
        functools.partial(gather_kernel, panel),
        out_shape=(jax.ShapeDtypeStruct(a_shape, jnp.bfloat16), jax.ShapeDtypeStruct(p_shape, jnp.bfloat16)),
        in_specs=[anywhere] * 2,
        out_specs=(anywhere, anywhere),
        scratch_shapes=[
            pltpu.VMEM(a_shape, jnp.bfloat16),
            pltpu.VMEM(p_shape, jnp.bfloat16),
            dma((SECTIONS, A_GROUPS * A_CUT)),
            dma((SECTIONS, 2)),
            dma((SECTIONS, 2)),
            dma((SECTIONS, 2, 3)),
            dma((SECTIONS, 2)),
        ]
        + ends * 4
        + [dma((2, SECTIONS)), dma((2,))],
        compiler_params=pltpu.CompilerParams(collective_id=1 + panel, has_side_effects=True, vmem_limit_bytes=16 * 1024 * 1024),
        name=f"gather_{panel}",
    )(a_blocks.reshape(2, A_GROUPS, 16, B * B), p_blocks.reshape(1, P_GROUPS, 16, B * B))


HALF = 512
PART = AGG_DEV * B


def add_rows(total, extra, count):
    @pl.loop(0, count)
    def _(i):
        total[i] = (total[i].astype(jnp.float32) + extra[i].astype(jnp.float32)).astype(jnp.bfloat16)


def reduce_kernel(t_ref, o_ref, own, fwd, in_a, in_b, mid, in2_a, in2_b, local_sem, send, recv, send2, recv2):
    y, z, x, core = place_of()
    y_next = [device((y + 1) % 4, z, x, core), device((y + 3) % 4, z, x, core)]
    z_next = [device(y, (z + 1) % 4, x, core), device(y, (z + 3) % 4, x, core)]
    greet(y_next + z_next)
    here = ((y, z), (z, y))
    nexts = ((y_next, z_next), (z_next, y_next))

    started = []
    for h in range(2):
        u = here[h][0]
        for d in range(2):
            step = (u + 1) % 4 if d == 0 else (u + 3) % 4
            copy = remote(t_ref.at[h, (u + 2) % 4, pl.ds(2 * d, 2)], in_a.at[h, d], send.at[h, d, 0], recv.at[h, d, 0], nexts[h][0][d])
            copy.start()
            started.append(copy)
    for h in range(2):
        u = here[h][0]
        for d in range(2):
            step = (u + 1) % 4 if d == 0 else (u + 3) % 4
            other = 2 * (1 - d)
            copy = remote(t_ref.at[h, step, pl.ds(other, 2)], in_b.at[h, d, pl.ds(other, 2)], send.at[h, d, 1], recv.at[h, d, 1], nexts[h][0][d])
            copy.start()
            started.append(copy)
            pltpu.make_async_copy(t_ref.at[h, step, pl.ds(2 * d, 2)], fwd.at[h, d], local_sem.at[h, d]).start()
        pltpu.make_async_copy(t_ref.at[h, u], own.at[h], local_sem.at[h, 2]).start()

    for h in range(2):
        u = here[h][0]
        for d in range(2):
            step = (u + 1) % 4 if d == 0 else (u + 3) % 4
            pltpu.make_async_copy(t_ref.at[h, step, pl.ds(2 * d, 2)], fwd.at[h, d], local_sem.at[h, d]).wait()
            remote(in_a.at[h, d], in_a.at[h, d], send.at[h, d, 0], recv.at[h, d, 0], nexts[h][0][d]).wait_recv()
            for part in range(2):
                add_rows(fwd.at[h, d, part], in_a.at[h, d, part], 4)
            copy = remote(fwd.at[h, d], in_b.at[h, d, pl.ds(2 * d, 2)], send.at[h, d, 2], recv.at[h, d, 2], nexts[h][0][d])
            copy.start()
            started.append(copy)

    def summed(h, part, i):
        first = own[h, part, i].astype(jnp.float32) + in_b[h, 0, part, i].astype(jnp.float32)
        return first + in_b[h, 1, part, i].astype(jnp.float32)

    for h in range(2):
        u, w = here[h]
        pltpu.make_async_copy(t_ref.at[h, u], own.at[h], local_sem.at[h, 2]).wait()
        for d in range(2):
            other = 2 * (1 - d)
            for part, index in ((other, 1), (2 * d, 2)):
                block = in_b.at[h, d, pl.ds(part, 2)]
                remote(block, block, send.at[h, d, index], recv.at[h, d, index], nexts[h][0][d]).wait_recv()

        opposite = (w + 2) % 4

        @pl.loop(0, 4)
        def _(i):
            mid[h, 2, i] = summed(h, opposite, i).astype(jnp.bfloat16)

        for d in range(2):
            copy = remote(mid.at[h, 2, pl.ds(2 * d, 2)], in2_a.at[h, d], send2.at[h, d, 0], recv2.at[h, d, 0], nexts[h][1][d])
            copy.start()
            started.append(copy)
        for d in range(2):
            step = (w + 1) % 4 if d == 0 else (w + 3) % 4
            other = 2 * (1 - d)

            @pl.loop(0, 2)
            def _(i):
                mid[h, d, other + i] = summed(h, step, other + i).astype(jnp.bfloat16)

            block = pl.ds(other, 2)
            copy = remote(mid.at[h, d, block], in2_b.at[h, d, block], send2.at[h, d, 1], recv2.at[h, d, 1], nexts[h][1][d])
            copy.start()
            started.append(copy)

    for h in range(2):
        u, w = here[h]
        for d in range(2):
            step = (w + 1) % 4 if d == 0 else (w + 3) % 4
            remote(in2_a.at[h, d], in2_a.at[h, d], send2.at[h, d, 0], recv2.at[h, d, 0], nexts[h][1][d]).wait_recv()

            @pl.loop(0, 2)
            def _(i):
                mid[h, d, 2 * d + i] = (summed(h, step, 2 * d + i) + in2_a[h, d, i].astype(jnp.float32)).astype(jnp.bfloat16)

            block = pl.ds(2 * d, 2)
            copy = remote(mid.at[h, d, block], in2_b.at[h, d, block], send2.at[h, d, 2], recv2.at[h, d, 2], nexts[h][1][d])
            copy.start()
            started.append(copy)

    for h in range(2):
        u, w = here[h]
        for d in range(2):
            other = 2 * (1 - d)
            for part, index in ((other, 1), (2 * d, 2)):
                block = in2_b.at[h, d, pl.ds(part, 2)]
                remote(block, block, send2.at[h, d, index], recv2.at[h, d, index], nexts[h][1][d]).wait_recv()

        @pl.loop(0, 4)
        def _(i):
            value = summed(h, w, i) + in2_b[h, 0, i].astype(jnp.float32) + in2_b[h, 1, i].astype(jnp.float32)
            o_ref[pl.ds(pl.multiple_of(i * B, B), B), h * HALF:(h + 1) * HALF] = value

    for copy in started:
        copy.wait_send()


def reduce_terms(term):
    return pl.pallas_call(
        reduce_kernel,
        out_shape=jax.ShapeDtypeStruct((PART, 2 * HALF), jnp.float32),
        in_specs=[pl.BlockSpec(memory_space=pl.ANY)],
        out_specs=pl.BlockSpec(memory_space=pltpu.VMEM),
        scratch_shapes=[
            pltpu.VMEM((2, 4, 4, B, HALF), jnp.bfloat16),
            pltpu.VMEM((2, 2, 2, 4, B, HALF), jnp.bfloat16),
            pltpu.VMEM((2, 2, 2, 4, B, HALF), jnp.bfloat16),
            pltpu.VMEM((2, 2, 4, 4, B, HALF), jnp.bfloat16),
            pltpu.VMEM((2, 3, 4, B, HALF), jnp.bfloat16),
            pltpu.VMEM((2, 2, 2, B, HALF), jnp.bfloat16),
            pltpu.VMEM((2, 2, 4, B, HALF), jnp.bfloat16),
            pltpu.SemaphoreType.DMA((2, 3)),
            pltpu.SemaphoreType.DMA((2, 2, 3)),
            pltpu.SemaphoreType.DMA((2, 2, 3)),
            pltpu.SemaphoreType.DMA((2, 2, 3)),
            pltpu.SemaphoreType.DMA((2, 2, 3)),
        ],
        compiler_params=pltpu.CompilerParams(collective_id=0, has_side_effects=True, vmem_limit_bytes=16 * 1024 * 1024),
        name="reduce_terms",
    )(term)


def halves(x, is_odd, keep):
    evens, odds = [], []
    for part in range(2):
        own = x[:, part * LANES:(part + 1) * LANES].astype(jnp.float32)
        swapped = pltpu.roll(own, 64, 1)
        evens.append(jnp.where(keep, jnp.where(is_odd, swapped, own), 0.0).astype(jnp.bfloat16))
        odds.append(jnp.where(keep, jnp.where(is_odd, own, swapped), 0.0).astype(jnp.bfloat16))
    return jnp.concatenate(evens, axis=1), jnp.concatenate(odds, axis=1)


def one_hot(position, count):
    rows = lax.broadcasted_iota(jnp.int32, (count, position.shape[1]), 0)
    return jnp.where(rows == position, 1.0, 0.0).astype(jnp.bfloat16)


def parity(cols):
    odd = (cols % 2).astype(jnp.float32)
    is_odd = jnp.broadcast_to(odd, (LANES, cols.shape[1])).T > 0.5
    lane = lax.broadcasted_iota(jnp.int32, is_odd.shape, 1)
    return is_odd, (lane < 64) != is_odd


def dot(a, b):
    return jnp.dot(a, b, preferred_element_type=jnp.float32)


UN_Q = 4
UN_I = 8


def local_kernel(sched, fine_agg, coarse_place, a_ref, p_ref, a_row, a_col, p_row, p_col, q_ref, cols_ref, out_ref,
                 a_dense, p_rows, p_dense, product, total, mask, q_rows):
    own_row = lax.axis_index("row")
    row_index = lax.broadcasted_iota(jnp.int32, (256, 256), 0)
    col_index = lax.broadcasted_iota(jnp.int32, (256, 256), 1)
    swap = jnp.where(col_index == (row_index % 16) * 16 + row_index // 16, 1.0, 0.0).astype(jnp.bfloat16)
    panels = (LAST, sched[0] + sched[1] - LAST)

    a_hot, a_par, p_hot, p_par = [], [], [], []
    for k in panels:
        pick = pl.ds(k, 1)
        a_hot.append(one_hot((a_col[pick, :] // 2) * FR + a_row[pick, :], 256))
        p_hot.append(one_hot((p_col[pick, :] // 2) * KB + p_row[pick, :], 128))
        a_par.append(parity(a_col[pick, :]))
        p_par.append(parity(p_col[pick, :]))

    block_of = (lax.broadcasted_iota(jnp.int32, (FR, CB * B), 1) // B).astype(jnp.float32)
    groups = cols_ref.shape[1]
    own = lax.broadcasted_iota(jnp.int32, (FR, groups), 1) == lax.broadcasted_iota(jnp.int32, (FR, groups), 0) + own_row * FR
    chosen = jnp.where(own, 1.0, 0.0).astype(jnp.bfloat16)
    picked = lax.dot_general(
        chosen, cols_ref[...].astype(jnp.float32).astype(jnp.bfloat16), (((1,), (1,)), ((), ())), preferred_element_type=jnp.float32
    )
    hit = block_of == picked[:, 0:1]
    for n in range(1, picked.shape[1]):
        hit = hit | (block_of == picked[:, n:n + 1])
    mask[...] = jnp.where(hit, 1.0, 0.0)
    for r in range(FR):
        q_rows[r * FR:(r + 1) * FR, :] = q_ref[:, r * LANES:(r + 1) * LANES].astype(jnp.float32)

    @pl.loop(0, 16, unroll=UN_Q)
    def _(q):
        lanes = pl.ds(pl.multiple_of(q * 256, 256), 256)
        for s in range(SECTIONS):
            parts = halves(p_ref[s, :, lanes], *p_par[s])
            for h in range(2):
                placed = dot(p_hot[s], parts[h]).astype(jnp.bfloat16)
                for part in range(2):
                    start = pl.multiple_of((q * 4 + part * 2 + h) * KB, KB)
                    for j in range(CB // 2):
                        p_rows[s, pl.ds(start, KB), j * LANES:(j + 1) * LANES] = placed[j * KB:(j + 1) * KB, part * LANES:(part + 1) * LANES]
            parts = halves(a_ref[s, :, lanes], *a_par[s])
            for h in range(2):
                placed = dot(a_hot[s], parts[h]).astype(jnp.bfloat16)
                for part in range(2):
                    start = pl.multiple_of((h * (B // 2) + q * 2 + part) * FR, FR)
                    for k in range(KB // 2):
                        lane = s * KB * B + k * LANES
                        a_dense[pl.ds(start, FR), lane:lane + LANES] = placed[k * FR:(k + 1) * FR, part * LANES:(part + 1) * LANES]

    for s in range(SECTIONS):
        for group in range(4):
            ordered = dot(swap, p_rows[s, group * 256:(group + 1) * 256, :]).astype(jnp.bfloat16)
            for k in range(KB):
                start = s * KB * B + k * B + group * 16
                p_dense[start:start + 16, :] = ordered[k * 16:(k + 1) * 16, :]

    for h in range(2):
        for n in range(2):

            @pl.loop(0, 4)
            def _(m):
                start = pl.multiple_of(m * 512, 512)
                lane = h * HALF + n * 256
                tile = dot(a_dense[pl.ds(start, 512), :], p_dense[:, lane:lane + 256])
                product[2 * n, pl.ds(start, 512), :] = tile[:, :LANES]
                product[2 * n + 1, pl.ds(start, 512), :] = tile[:, LANES:]

        @pl.loop(0, 64)
        def _(g):
            total[g] = jnp.zeros((B, HALF), jnp.float32)

        @pl.loop(0, FR, step=UN_I)
        def _(first):
            terms = []
            turned = []
            for t in range(4):
                groups = []
                for high in range(B // 8):
                    rows = [product[t, pl.ds(pl.multiple_of((high * 8 + low) * FR + first, 8), 8), :] for low in range(8)]
                    groups.append(jnp.swapaxes(jnp.stack(rows, axis=0), 0, 1))
                turned.append(groups)
            for u in range(UN_I):
                i = first + u
                pair = q_rows[pl.ds(i, B // 2, stride=FR), :]
                flipped = jnp.concatenate([pair, pltpu.roll(pair, 64, 1)], axis=0)[:, :B]
                lhs = jnp.concatenate([flipped, flipped], axis=0).astype(jnp.bfloat16)
                for j in range(0, 4, 2):
                    tops, bottoms = [], []
                    for t in (j, j + 1):
                        block = jnp.concatenate([group[u] for group in turned[t]], axis=0)
                        top = block.astype(jnp.bfloat16)
                        tops.append(top)
                        bottoms.append((block - top.astype(jnp.float32)).astype(jnp.bfloat16))
                    rhs = jnp.concatenate([jnp.concatenate(tops, axis=1), jnp.concatenate(bottoms, axis=1)], axis=0)
                    term = lax.dot_general(lhs, rhs, (((0,), (0,)), ((), ())), preferred_element_type=jnp.float32)
                    terms.append(term.astype(jnp.bfloat16).astype(jnp.float32))
            for u in range(UN_I):
                i = first + u
                place = coarse_place[fine_agg[own_row * FR + i]]
                owner, member = place // AGG_DEV, place % AGG_DEV
                target = place if h == 0 else ((owner % 4) * 4 + owner // 4) * AGG_DEV + member
                for j in range(0, 4, 2):
                    lanes = slice(j * LANES, (j + 2) * LANES)
                    keep = mask[pl.ds(i, 1), h * HALF + j * LANES:h * HALF + (j + 2) * LANES]
                    total[target, :, lanes] += terms[u * 2 + j // 2] * keep

        @pl.loop(0, 64)
        def _(g):
            out_ref[h, g] = total[g].astype(jnp.bfloat16)


def local_terms(sched, fine_agg, coarse_place, a, p, a_row, a_col, p_row, p_col, q, prod_cols):
    smem = pl.BlockSpec(memory_space=pltpu.SMEM)
    vmem = pl.BlockSpec(memory_space=pltpu.VMEM)
    return pl.pallas_call(
        local_kernel,
        out_shape=jax.ShapeDtypeStruct((2, 64, B, HALF), jnp.bfloat16),
        in_specs=[smem] * 3 + [vmem] * 8,
        out_specs=vmem,
        scratch_shapes=[
            pltpu.VMEM((FR * B, SECTIONS * KB * B), jnp.bfloat16),
            pltpu.VMEM((SECTIONS, KB * B, CB * B), jnp.bfloat16),
            pltpu.VMEM((SECTIONS * KB * B, CB * B), jnp.bfloat16),
            pltpu.VMEM((4, FR * B, LANES), jnp.float32),
            pltpu.VMEM((64, B, HALF), jnp.float32),
            pltpu.VMEM((FR, CB * B), jnp.float32),
            pltpu.VMEM((FR * B // 2, LANES), jnp.float32),
        ],
        compiler_params=pltpu.CompilerParams(vmem_limit_bytes=44 * 1024 * 1024),
        name="local_terms",
    )(sched, fine_agg, coarse_place, a, p, a_row, a_col, p_row, p_col, q, prod_cols)


def per_device(a_blocks, a_row, a_col, p_blocks, p_row, p_col, q_blocks, sched, fine_agg, coarse_place, prod_cols):
    other = jnp.sum(sched) - LAST
    a, p = lax.switch(other, [functools.partial(gather_panels, k) for k in range(LAST)], a_blocks, p_blocks)
    term = local_terms(
        sched,
        fine_agg,
        coarse_place,
        a.reshape(SECTIONS, FR * 8, B * B),
        p.reshape(SECTIONS, KB * 8, B * B),
        a_row,
        a_col,
        p_row,
        p_col,
        q_blocks,
        prod_cols.T,
    )
    return reduce_terms(term.reshape(2, 4, 4, 4, B, HALF))


def solution(mesh):
    in_specs = (
        P("col", "row", None),
        P(None, "row"),
        P(None, "row"),
        P("row", "col", None),
        P(None, "col"),
        P(None, "col"),
        P("row", None),
        P(),
        P(),
        P(),
        P(None, "col"),
    )
    return jax.shard_map(per_device, mesh=mesh, in_specs=in_specs, out_specs=P("row", "col"), check_vma=False)
```
